256 devices in a mesh: req: 16 (over y, x), kv: 2 (over core), hid: 8 (over z).
Axes of the slice: x: 4, y: 4, z: 8, core: 2. Of those that a mesh axis runs over, the one named last changes fastest.
Arguments:
- tokens: bfloat16 [64, 8, 2048], P('req', 'hid'), may hold values from -6 to 6
- gains: float32 [4, 2048], replicated, may hold values from 0.1 to 1.9
- qk_gains: float32 [2, 256], replicated, may hold values from 0.1 to 1.9
- w_query: bfloat16 [2048, 2048], P('req', 'kv'), may hold values from -0.125 to 0.125
- key_value_weight: bfloat16 [2048, 2, 512], P('req', None, 'kv'), may hold values from -0.125 to 0.125
- output_weight: bfloat16 [2, 1024, 2048], P('kv', 'req'), may hold values from -0.125 to 0.125
- w_gateup: bfloat16 [2048, 2, 8192], P(None, None, ('kv', 'hid')), may hold values from -0.125 to 0.125
- w_down: bfloat16 [8192, 2048], P(('kv', 'hid')), may hold values from -0.0625 to 0.0625
- kv_cache: bfloat16 [5504, 2, 64, 512], P(('req', 'hid'), None, None, 'kv'), may hold values from -128 to 128
- lengths: int32 [64, 8], replicated, may hold values from 1 to 2048, as said below
- page_table: int32 [64, 8, 32], replicated, may hold values from -1 to 5503, as said below
Outputs:
- result: bfloat16 [64, 8, 2048], P(('req', 'kv'), 'hid')
The draws below stay inside these ranges and needn't reach their ends.
Inputs may be any that keep to these rules, and one draw needn't show every extreme that they name: Request (j, g) belongs to tenant j % 4, whose lengths lie in max(1, c // 4) to c with c = 64, 128, 256 and 2048 for tenants 0 to 3. `page_table`: all pages of request (j, g) lie in one pool of its group: slots (r * 8 + g) * 43 to (r * 8 + g + 1) * 43 - 1 for one r; every pool holds the pages of 4 requests of its group, 1 of each tenant; entry p is -1 exactly where p * 64 >= lengths[j, g]; no slot is used twice.
All inputs are finite; a program needn't handle non-finite values.
Results may differ from the reference program's by a relative error of at most 0.035.
Values may be sent and summed in bfloat16 or wider, within the bound.
A program may use at most 64 MiB of HBM per device.

```python
import jax
import jax.numpy as jnp
from jax import lax

MODEL_DIM = 2048
QUERY_COUNT = 8
KEY_HEADS = 2
HEAD_SIZE = 256
FF = 8192
PAGE_LENGTH = 64
MAXLEN = 2048
RQ_DEV = 4
RH = 64
GROUPS = 8
PMAX = 32
POOL = 43
PAGE_COUNT = 5504


def layout(key):
    folded = jax.random.fold_in(key, 11)
    rank_key, length_key, pool_key = jax.random.split(folded, 3)
    member_count = RH // 4
    per_tenant = RQ_DEV // 4
    scores = jax.random.randint(rank_key, (GROUPS, 4, member_count), 0, 65536) * member_count + jnp.arange(member_count, dtype=jnp.int32)
    order_rank = jnp.argsort(jnp.argsort(scores, axis=-1), axis=-1).astype(jnp.int32)
    request_ids = jnp.arange(RH, dtype=jnp.int32)
    tenant = request_ids % 4
    member = request_ids // 4
    holder = order_rank[:, tenant, member] // per_tenant
    divisor = jnp.array([32, 16, 8, 1], dtype=jnp.int32)[tenant]
    length_cap = MAXLEN // divisor
    length_low = jnp.maximum(1, length_cap // 4)
    length = jax.random.randint(length_key, (GROUPS, RH), length_low[None, :], length_cap[None, :] + 1).astype(jnp.int32)
    length = length.at[0, 3].set(MAXLEN)
    page_counts = (length + PAGE_LENGTH - 1) // PAGE_LENGTH
    earlier_same = (holder[:, :, None] == holder[:, None, :]) & (request_ids[None, None, :] < request_ids[None, :, None])
    offset = jnp.sum(jnp.where(earlier_same, page_counts[:, None, :], 0), axis=2)
    pool_scores = jax.random.randint(pool_key, (GROUPS, RH // RQ_DEV, POOL), 0, 65536) * POOL + jnp.arange(POOL, dtype=jnp.int32)
    shuffle = jnp.argsort(pool_scores, axis=-1).astype(jnp.int32)
    page_ids = jnp.arange(PMAX, dtype=jnp.int32)
    position = jnp.minimum(offset[:, :, None] + page_ids, POOL - 1)
    holder_shuffle = shuffle[jnp.arange(GROUPS, dtype=jnp.int32)[:, None], holder]
    slot_local = jnp.take_along_axis(holder_shuffle, position, axis=2)
    slot_table = (holder[:, :, None] * GROUPS + jnp.arange(GROUPS, dtype=jnp.int32)[:, None, None]) * POOL + slot_local
    slot_table = jnp.where(page_ids < page_counts[:, :, None], slot_table, -1).astype(jnp.int32)
    return (jnp.transpose(length, (1, 0)), jnp.transpose(slot_table, (1, 0, 2)))


def draw_lengths(key, part):
    return layout(key)[0]


def draw_page_table(key, part):
    return layout(key)[1]


def draw_kv_cache(key, part):
    random_noise_key = jax.random.fold_in(jax.random.fold_in(key, 23), 0)
    value_entries = jax.random.normal(random_noise_key, (PAGE_COUNT, 2, PAGE_LENGTH, KEY_HEADS * HEAD_SIZE), jnp.float32)
    return jnp.clip(value_entries, -128.0, 128.0).astype(jnp.bfloat16)


def shard_levels(key, dims, cuts, least, largest):
    def one(dim, parts):
        draws = jax.random.uniform(jax.random.fold_in(jax.random.fold_in(key, 6), dim), (parts,), jnp.float32, least / len(cuts), largest / len(cuts))
        return jnp.repeat(jnp.exp(draws), dims[dim] // parts).reshape((-1,) + (1,) * (len(dims) - dim - 1))

    loudness = one(*cuts[0])
    for cut in cuts[1:]:
        loudness = loudness * one(*cut)
    return loudness


def gaussian(rng, shape, scale, bound, shards=(), kind=jnp.bfloat16):
    values = scale * jax.random.normal(rng, shape, jnp.float32)
    if shards:
        values = values * shard_levels(rng, shape, shards, -0.22, 0.18)
    return jnp.clip(values, -bound, bound).astype(kind)


def setup_inputs(seed: int = 0) -> dict:
    key_list = jax.random.split(jax.random.key(seed), 12)
    return {
        "tokens": gaussian(key_list[0], (RH, GROUPS, MODEL_DIM), 1.0, 6.0, ((0, 16), (1, 8))),
        "gains": jnp.clip(1.0 + 0.18 * jax.random.normal(key_list[1], (4, MODEL_DIM), jnp.float32), 0.1, 1.9),
        "qk_gains": jnp.clip(1.0 + 0.18 * jax.random.normal(key_list[2], (2, HEAD_SIZE), jnp.float32), 0.1, 1.9),
        "w_query": gaussian(key_list[3], (MODEL_DIM, QUERY_COUNT * HEAD_SIZE), MODEL_DIM ** -0.5, 0.125, ((0, 16), (1, 2))),
        "key_value_weight": gaussian(key_list[4], (MODEL_DIM, 2, KEY_HEADS * HEAD_SIZE), MODEL_DIM ** -0.5, 0.125, ((0, 16), (2, 2))),
        "output_weight": gaussian(key_list[5], (KEY_HEADS, QUERY_COUNT // KEY_HEADS * HEAD_SIZE, MODEL_DIM), (QUERY_COUNT * HEAD_SIZE) ** -0.5, 0.125, ((0, 2), (1, 16))),
        "w_gateup": gaussian(key_list[6], (MODEL_DIM, 2, FF), MODEL_DIM ** -0.5, 0.125, ((2, 16),)),
        "w_down": gaussian(key_list[7], (FF, MODEL_DIM), FF ** -0.5, 0.0625, ((0, 16),)),
        "kv_cache": draw_kv_cache(jax.random.fold_in(key_list[11], 71), 0),
        "lengths": draw_lengths(jax.random.fold_in(key_list[11], 71), 0),
        "page_table": draw_page_table(jax.random.fold_in(key_list[11], 71), 0),
    }


eps_norm = 1e-06
rope_base = 1000000.0
neg_large = -1e+30

def rms_scale(value_entries, gain_row):
    mean_square = lax.optimization_barrier(jnp.mean(value_entries * value_entries, axis=-1, keepdims=True))
    return value_entries * lax.rsqrt(mean_square + eps_norm) * gain_row

def rotate(value_entries, position):
    half_width = value_entries.shape[-1] // 2
    frequency = rope_base ** (-jnp.arange(half_width, dtype=jnp.float32) * 2.0 / value_entries.shape[-1])
    angles = position[:, None, None] * frequency
    cosines = jnp.cos(angles)
    sines = jnp.sin(angles)
    first_half = value_entries[..., :half_width]
    second_half = value_entries[..., half_width:]
    return jnp.concatenate([first_half * cosines - second_half * sines, second_half * cosines + first_half * sines], axis=-1)

def reference(tokens, gains, qk_gains, w_query, key_value_weight, output_weight, w_gateup, w_down, kv_cache, lengths, page_table):
    request_total, group_total, model_width = tokens.shape
    request_count = request_total * group_total
    flat_rows = tokens.reshape(request_count, model_width).astype(jnp.float32)
    normed = rms_scale(flat_rows, gains[0]).astype(jnp.bfloat16)
    head_width = qk_gains.shape[1]
    kv_heads = key_value_weight.shape[2] // head_width
    query_heads = w_query.shape[1] // head_width
    per_group = query_heads // kv_heads
    query_sum = jnp.dot(normed, w_query, preferred_element_type=jnp.float32)
    keyval_sum = jnp.dot(normed, key_value_weight.reshape(model_width, -1), preferred_element_type=jnp.float32)
    flat_lengths = lengths.reshape(request_count).astype(jnp.int32)
    position = flat_lengths.astype(jnp.float32)
    query = rotate(rms_scale(query_sum.reshape(request_count, query_heads, head_width), qk_gains[0]), position).astype(jnp.bfloat16)
    key_part = keyval_sum[:, :kv_heads * head_width].reshape(request_count, kv_heads, head_width)
    key_new = rotate(rms_scale(key_part, qk_gains[1]), position).astype(jnp.bfloat16)
    value_part = keyval_sum[:, kv_heads * head_width:].reshape(request_count, kv_heads, head_width)
    value_new = rms_scale(value_part, 1.0).astype(jnp.bfloat16)
    flat_tables = page_table.reshape(request_count, -1).astype(jnp.int32)
    scale_factor = head_width ** (-0.5)

    def single_request(inputs):
        query_row, key_row, value_row, table_row, length = inputs
        clamped = jnp.maximum(table_row, 0).astype(jnp.int32)
        pages = kv_cache[clamped]
        page_total, _, page_size, _ = pages.shape
        cached_keys = pages[:, 0].reshape(page_total * page_size, kv_heads, head_width).astype(jnp.float32)
        cached_values = pages[:, 1].reshape(page_total * page_size, kv_heads, head_width).astype(jnp.float32)
        query_heads_f = query_row.reshape(kv_heads, per_group, head_width).astype(jnp.float32)
        scores = jnp.einsum('ghd,tgd->ght', query_heads_f, cached_keys) * scale_factor
        live_mask = jnp.arange(page_total * page_size, dtype=jnp.int32) < length
        masked = jnp.where(live_mask, scores, neg_large)
        highest_cached = lax.optimization_barrier(jnp.max(masked, axis=2))
        weights = jnp.where(live_mask, jnp.exp(masked - highest_cached[..., None]), 0.0)
        totals = lax.optimization_barrier(jnp.sum(weights, axis=2))
        rounded = lax.optimization_barrier(weights.astype(jnp.bfloat16))
        weighted = jnp.einsum('ght,tgd->ghd', rounded.astype(jnp.float32), cached_values)
        own_score = lax.optimization_barrier(jnp.sum(query_heads_f * key_row.astype(jnp.float32)[:, None, :], axis=-1)) * scale_factor
        highest = jnp.maximum(highest_cached, own_score)
        old_scale = jnp.exp(highest_cached - highest)
        new_scale = jnp.exp(own_score - highest)
        combined = (weighted * old_scale[..., None] + new_scale[..., None] * value_row.astype(jnp.float32)[:, None, :]) / (totals * old_scale + new_scale)[..., None]
        return combined.reshape(query_heads, head_width).astype(jnp.bfloat16)
    attended = lax.map(single_request, (query, key_new, value_new, flat_tables, flat_lengths))
    projected = jnp.dot(attended.reshape(request_count, -1), output_weight.reshape(-1, model_width), preferred_element_type=jnp.float32)
    middle = (flat_rows + rms_scale(projected, gains[1])).astype(jnp.bfloat16)
    ffn_input = rms_scale(middle.astype(jnp.float32), gains[2]).astype(jnp.bfloat16)
    gate_value = jnp.dot(ffn_input, w_gateup[:, 0, :], preferred_element_type=jnp.float32)
    up_value = jnp.dot(ffn_input, w_gateup[:, 1, :], preferred_element_type=jnp.float32)
    hidden = (jax.nn.gelu(gate_value, approximate=True) * up_value).astype(jnp.bfloat16)
    ffn_sum = jnp.dot(hidden, w_down, preferred_element_type=jnp.float32)
    result = (middle.astype(jnp.float32) + rms_scale(ffn_sum, gains[3])).astype(jnp.bfloat16)
    return result.reshape(request_total, group_total, model_width)
```

```python
import functools

import jax
import jax.numpy as jnp
from jax import lax
from jax.experimental import pallas as pl
from jax.experimental.pallas import tpu as pltpu
from jax.sharding import PartitionSpec as P

eps_norm = 1e-06
rope_base = 1000000.0
neg_large = -1e30
MESH = pl.DeviceIdType.MESH
AXES = ("req", "kv", "hid")


def group_layout(group):
    sizes = [lax.axis_size(a) for a in group]
    me = 0
    for a, s in zip(group, sizes):
        me = me * s + lax.axis_index(a)
    total = 1
    for s in sizes:
        total *= s
    return sizes, me, total


def device_of(group, sizes, position):
    coords = {a: lax.axis_index(a) for a in AXES}
    rest = position
    for a, s in reversed(list(zip(group, sizes))):
        coords[a] = rest % s
        rest = rest // s
    return tuple(coords[a] for a in AXES)


def exchange_kernel(group, bcast, x_ref, y_ref, send_sem, recv_sem):
    sizes, me, n = group_layout(group)
    barrier = pltpu.get_barrier_semaphore()
    for s in range(1, n):
        peer = lax.rem(me + s, n)
        pl.semaphore_signal(
            barrier, inc=1, device_id=device_of(group, sizes, peer), device_id_type=MESH
        )
    pl.semaphore_wait(barrier, n - 1)
    copies = []
    for s in range(1, n):
        peer = lax.rem(me + s, n)
        src = x_ref if bcast else x_ref.at[peer]
        copy = pltpu.make_async_remote_copy(
            src_ref=src,
            dst_ref=y_ref.at[me],
            send_sem=send_sem.at[s],
            recv_sem=recv_sem.at[s],
            device_id=device_of(group, sizes, peer),
            device_id_type=MESH,
        )
        copy.start()
        copies.append(copy)
    if bcast:
        y_ref[me] = x_ref[...]
    else:
        y_ref[me] = x_ref[me]
    for s in range(1, n):
        copies[s - 1].wait_send()
        origin = lax.rem(me + n - s, n)
        src = x_ref if bcast else x_ref.at[origin]
        pltpu.make_async_remote_copy(
            src_ref=src,
            dst_ref=y_ref.at[origin],
            send_sem=send_sem.at[s],
            recv_sem=recv_sem.at[s],
            device_id=device_of(group, sizes, origin),
            device_id_type=MESH,
        ).wait_recv()


def exchange(x, group, cid, bcast=False):
    n = 1
    for a in group:
        n *= lax.axis_size(a)
    block = x.shape if bcast else x.shape[1:]
    return pl.pallas_call(
        functools.partial(exchange_kernel, group, bcast),
        out_shape=jax.ShapeDtypeStruct((n,) + tuple(block), x.dtype),
        in_specs=[pl.BlockSpec(memory_space=pltpu.VMEM)],
        out_specs=pl.BlockSpec(memory_space=pltpu.VMEM),
        scratch_shapes=[pltpu.SemaphoreType.DMA((n,)), pltpu.SemaphoreType.DMA((n,))],
        compiler_params=pltpu.CompilerParams(collective_id=cid, has_side_effects=True),
    )(x)


def rms_scale(value_entries, gain_row):
    mean_square = jnp.mean(value_entries * value_entries, axis=-1, keepdims=True)
    return value_entries * lax.rsqrt(mean_square + eps_norm) * gain_row


def rotate(value_entries, position):
    half_width = value_entries.shape[-1] // 2
    frequency = rope_base ** (
        -jnp.arange(half_width, dtype=jnp.float32) * 2.0 / value_entries.shape[-1]
    )
    angles = position[:, None, None] * frequency
    cosines = jnp.cos(angles)
    sines = jnp.sin(angles)
    first_half = value_entries[..., :half_width]
    second_half = value_entries[..., half_width:]
    return jnp.concatenate(
        [first_half * cosines - second_half * sines, second_half * cosines + first_half * sines],
        axis=-1,
    )


def shards(
    tokens,
    gains,
    qk_gains,
    w_query,
    key_value_weight,
    output_weight,
    w_gateup,
    w_down,
    kv_cache,
    lengths,
    page_table,
):
    req_position = lax.axis_index("req")
    kv_position = lax.axis_index("kv")
    hid_position = lax.axis_index("hid")
    req_total = lax.axis_size("req")
    hid_total = lax.axis_size("hid")
    kv_total = lax.axis_size("kv")
    rows_here, _, model_width = tokens.shape
    half_rows = rows_here // kv_total
    head_width = qk_gains.shape[1]
    per_group = w_query.shape[1] // head_width
    pool_size, _, page_size, _ = kv_cache.shape
    request_count = rows_here * req_total
    feature_width = w_query.shape[0]

    own_rows = tokens[:, 0, :].astype(jnp.float32)
    normed = rms_scale(own_rows, gains[0]).astype(jnp.bfloat16)

    send_tokens = normed.reshape(rows_here, req_total, feature_width).transpose(1, 0, 2)
    columns = exchange(send_tokens, ("req",), 0).reshape(request_count, feature_width)

    group_lengths = lax.dynamic_index_in_dim(lengths, hid_position, axis=1, keepdims=False)
    group_table = lax.dynamic_index_in_dim(page_table, hid_position, axis=1, keepdims=False)
    request_ids = jnp.arange(request_count, dtype=jnp.int32)
    pool_of = (group_table[:, 0] // pool_size) // hid_total
    pool_pos = pool_of * rows_here + request_ids % rows_here
    order = pool_pos[None, :] == request_ids[:, None]
    order_b = order.astype(jnp.bfloat16)
    columns_pooled = jnp.dot(order_b, columns, preferred_element_type=jnp.float32).astype(
        jnp.bfloat16
    )

    projection = jnp.concatenate(
        [w_query, key_value_weight.reshape(key_value_weight.shape[0], -1)], axis=1
    )
    partial = jnp.dot(columns_pooled, projection, preferred_element_type=jnp.float32)
    gathered = exchange(partial.reshape(req_total, rows_here, -1), ("req",), 1)
    summed = jnp.sum(gathered, axis=0)

    mine = lax.dynamic_slice_in_dim(order, req_position * rows_here, rows_here, 0)
    my_lengths = jnp.sum(jnp.where(mine, group_lengths[None, :], 0), axis=1)
    my_tables = jnp.sum(jnp.where(mine[:, :, None], group_table[None, :, :], 0), axis=1)

    position = my_lengths.astype(jnp.float32)
    split_at = per_group * head_width
    query = summed[:, :split_at].reshape(rows_here, per_group, head_width)
    query = rotate(rms_scale(query, qk_gains[0]), position).astype(jnp.bfloat16)
    key_part = summed[:, split_at : split_at + head_width][:, None, :]
    key_new = rotate(rms_scale(key_part, qk_gains[1]), position)[:, 0].astype(jnp.bfloat16)
    value_new = rms_scale(summed[:, split_at + head_width :], 1.0).astype(jnp.bfloat16)

    slot_base = (req_position * hid_total + hid_position) * pool_size
    local = my_tables - slot_base
    slots = jnp.arange(pool_size, dtype=jnp.int32)
    match = local[:, :, None] == slots[None, None, :]
    page_ids = jnp.arange(my_tables.shape[1], dtype=jnp.int32)
    owner_hit = jnp.any(match, axis=1)
    page_of = jnp.sum(jnp.where(match, page_ids[None, :, None], 0), axis=(0, 1))
    cache_pos = page_of[:, None] * page_size + jnp.arange(page_size, dtype=jnp.int32)[None, :]
    live = owner_hit[:, :, None] & (cache_pos[None] < my_lengths[:, None, None])
    live = live.reshape(rows_here, 1, pool_size * page_size)

    cached_keys = kv_cache[:, 0].reshape(pool_size * page_size, head_width)
    cached_values = kv_cache[:, 1].reshape(pool_size * page_size, head_width)
    scale_factor = head_width ** (-0.5)
    scores = jnp.dot(
        query.reshape(rows_here * per_group, head_width),
        cached_keys.T,
        preferred_element_type=jnp.float32,
    ).reshape(rows_here, per_group, -1) * scale_factor
    masked = jnp.where(live, scores, neg_large)
    highest_cached = jnp.max(masked, axis=2)
    weights = jnp.where(live, jnp.exp(masked - highest_cached[..., None]), 0.0)
    totals = jnp.sum(weights, axis=2)
    weighted = jnp.dot(
        weights.astype(jnp.bfloat16).reshape(rows_here * per_group, -1),
        cached_values,
        preferred_element_type=jnp.float32,
    ).reshape(rows_here, per_group, head_width)
    query_f = query.astype(jnp.float32)
    own_score = jnp.sum(query_f * key_new.astype(jnp.float32)[:, None, :], axis=-1) * scale_factor
    highest = jnp.maximum(highest_cached, own_score)
    old_scale = jnp.exp(highest_cached - highest)
    new_scale = jnp.exp(own_score - highest)
    combined = (
        weighted * old_scale[..., None]
        + new_scale[..., None] * value_new.astype(jnp.float32)[:, None, :]
    ) / (totals * old_scale + new_scale)[..., None]
    attended = combined.astype(jnp.bfloat16).reshape(rows_here, per_group * head_width)

    slice_width = output_weight.shape[1]
    send_att = attended.reshape(rows_here, req_total, slice_width).transpose(1, 0, 2)
    got_att = exchange(send_att, ("req",), 2).reshape(request_count, slice_width)
    att_natural = jnp.dot(order_b.T, got_att, preferred_element_type=jnp.float32).astype(
        jnp.bfloat16
    )
    proj_partial = jnp.dot(att_natural, output_weight[0], preferred_element_type=jnp.float32)
    proj_partial = proj_partial.astype(jnp.bfloat16).reshape(
        req_total * kv_total, half_rows, model_width
    )
    projected = jnp.sum(
        exchange(proj_partial, ("req", "kv"), 3).astype(jnp.float32), axis=0
    )

    residual = lax.dynamic_slice_in_dim(own_rows, kv_position * half_rows, half_rows, 0)
    middle = (residual + rms_scale(projected, gains[1])).astype(jnp.bfloat16)
    ffn_input = rms_scale(middle.astype(jnp.float32), gains[2]).astype(jnp.bfloat16)
    ffn_rows = exchange(ffn_input, ("kv", "hid"), 4, bcast=True).reshape(-1, model_width)
    gate_up = jnp.einsum(
        "nd,dgf->ngf", ffn_rows, w_gateup, preferred_element_type=jnp.float32
    )
    hidden = (jax.nn.gelu(gate_up[:, 0], approximate=True) * gate_up[:, 1]).astype(jnp.bfloat16)
    ffn_partial = jnp.dot(hidden, w_down, preferred_element_type=jnp.float32).astype(
        jnp.bfloat16
    )
    ffn_partial = ffn_partial.reshape(kv_total * hid_total, half_rows, model_width)
    ffn_sum = jnp.sum(exchange(ffn_partial, ("kv", "hid"), 5).astype(jnp.float32), axis=0)
    result = (middle.astype(jnp.float32) + rms_scale(ffn_sum, gains[3])).astype(jnp.bfloat16)
    return result[:, None, :]


def solution(mesh):
    return jax.shard_map(
        shards,
        mesh=mesh,
        in_specs=(
            P("req", "hid", None),
            P(),
            P(),
            P("req", "kv"),
            P("req", None, "kv"),
            P("kv", "req", None),
            P(None, None, ("kv", "hid")),
            P(("kv", "hid"), None),
            P(("req", "hid"), None, None, "kv"),
            P(),
            P(),
        ),
        out_specs=P(("req", "kv"), "hid", None),
        check_vma=False,
    )
```

```python
import functools

import jax
import jax.numpy as jnp
from jax import lax
from jax.experimental import pallas as pl
from jax.experimental.pallas import tpu as pltpu
from jax.sharding import PartitionSpec as P

eps_norm = 1e-06
rope_base = 1000000.0
neg_large = -1e30
MESH = pl.DeviceIdType.MESH
AXES = ("req", "kv", "hid")


def group_layout(group):
    sizes = [lax.axis_size(a) for a in group]
    me = 0
    for a, s in zip(group, sizes):
        me = me * s + lax.axis_index(a)
    total = 1
    for s in sizes:
        total *= s
    return sizes, me, total


def device_of(group, sizes, position):
    coords = {a: lax.axis_index(a) for a in AXES}
    rest = position
    for a, s in reversed(list(zip(group, sizes))):
        coords[a] = rest % s
        rest = rest // s
    return tuple(coords[a] for a in AXES)


def exchange_kernel(group, bcast, x_ref, y_ref, send_sem, recv_sem):
    sizes, me, n = group_layout(group)
    barrier = pltpu.get_barrier_semaphore()
    for s in range(1, n):
        peer = lax.rem(me + s, n)
        pl.semaphore_signal(
            barrier, inc=1, device_id=device_of(group, sizes, peer), device_id_type=MESH
        )
    pl.semaphore_wait(barrier, n - 1)
    copies = []
    for s in range(1, n):
        peer = lax.rem(me + s, n)
        src = x_ref if bcast else x_ref.at[peer]
        copy = pltpu.make_async_remote_copy(
            src_ref=src,
            dst_ref=y_ref.at[me],
            send_sem=send_sem.at[s],
            recv_sem=recv_sem.at[s],
            device_id=device_of(group, sizes, peer),
            device_id_type=MESH,
        )
        copy.start()
        copies.append(copy)
    if bcast:
        y_ref[me] = x_ref[...]
    else:
        y_ref[me] = x_ref[me]
    for s in range(1, n):
        copies[s - 1].wait_send()
        origin = lax.rem(me + n - s, n)
        src = x_ref if bcast else x_ref.at[origin]
        pltpu.make_async_remote_copy(
            src_ref=src,
            dst_ref=y_ref.at[origin],
            send_sem=send_sem.at[s],
            recv_sem=recv_sem.at[s],
            device_id=device_of(group, sizes, origin),
            device_id_type=MESH,
        ).wait_recv()


def exchange(x, group, cid, bcast=False):
    if not bcast:
        return lax.all_to_all(x, group, 0, 0, tiled=True)
    n = 1
    for a in group:
        n *= lax.axis_size(a)
    block = x.shape if bcast else x.shape[1:]
    return pl.pallas_call(
        functools.partial(exchange_kernel, group, bcast),
        out_shape=jax.ShapeDtypeStruct((n,) + tuple(block), x.dtype),
        in_specs=[pl.BlockSpec(memory_space=pltpu.VMEM)],
        out_specs=pl.BlockSpec(memory_space=pltpu.VMEM),
        scratch_shapes=[pltpu.SemaphoreType.DMA((n,)), pltpu.SemaphoreType.DMA((n,))],
        compiler_params=pltpu.CompilerParams(collective_id=cid, has_side_effects=True),
    )(x)


def rms_scale(value_entries, gain_row):
    mean_square = jnp.mean(value_entries * value_entries, axis=-1, keepdims=True)
    return value_entries * lax.rsqrt(mean_square + eps_norm) * gain_row


def rotate(value_entries, position):
    half_width = value_entries.shape[-1] // 2
    frequency = rope_base ** (
        -jnp.arange(half_width, dtype=jnp.float32) * 2.0 / value_entries.shape[-1]
    )
    angles = position[:, None, None] * frequency
    cosines = jnp.cos(angles)
    sines = jnp.sin(angles)
    first_half = value_entries[..., :half_width]
    second_half = value_entries[..., half_width:]
    return jnp.concatenate(
        [first_half * cosines - second_half * sines, second_half * cosines + first_half * sines],
        axis=-1,
    )


def shards(
    tokens,
    gains,
    qk_gains,
    w_query,
    key_value_weight,
    output_weight,
    w_gateup,
    w_down,
    kv_cache,
    lengths,
    page_table,
):
    req_position = lax.axis_index("req")
    kv_position = lax.axis_index("kv")
    hid_position = lax.axis_index("hid")
    req_total = lax.axis_size("req")
    hid_total = lax.axis_size("hid")
    kv_total = lax.axis_size("kv")
    rows_here, _, model_width = tokens.shape
    half_rows = rows_here // kv_total
    head_width = qk_gains.shape[1]
    per_group = w_query.shape[1] // head_width
    pool_size, _, page_size, _ = kv_cache.shape
    request_count = rows_here * req_total
    feature_width = w_query.shape[0]

    own_rows = tokens[:, 0, :].astype(jnp.float32)
    normed = rms_scale(own_rows, gains[0]).astype(jnp.bfloat16)

    send_tokens = normed.reshape(rows_here, req_total, feature_width).transpose(1, 0, 2)
    columns = exchange(send_tokens, ("req",), 0).reshape(request_count, feature_width)

    group_lengths = lax.dynamic_index_in_dim(lengths, hid_position, axis=1, keepdims=False)
    group_table = lax.dynamic_index_in_dim(page_table, hid_position, axis=1, keepdims=False)
    request_ids = jnp.arange(request_count, dtype=jnp.int32)
    pool_of = (group_table[:, 0] // pool_size) // hid_total
    pool_pos = pool_of * rows_here + request_ids % rows_here
    order = pool_pos[None, :] == request_ids[:, None]
    order_b = order.astype(jnp.bfloat16)
    columns_pooled = jnp.dot(order_b, columns, preferred_element_type=jnp.float32).astype(
        jnp.bfloat16
    )

    projection = jnp.concatenate(
        [w_query, key_value_weight.reshape(key_value_weight.shape[0], -1)], axis=1
    )
    partial = jnp.dot(columns_pooled, projection, preferred_element_type=jnp.float32)
    gathered = exchange(partial.reshape(req_total, rows_here, -1), ("req",), 1)
    summed = jnp.sum(gathered, axis=0)

    mine = lax.dynamic_slice_in_dim(order, req_position * rows_here, rows_here, 0)
    my_lengths = jnp.sum(jnp.where(mine, group_lengths[None, :], 0), axis=1)
    my_tables = jnp.sum(jnp.where(mine[:, :, None], group_table[None, :, :], 0), axis=1)

    position = my_lengths.astype(jnp.float32)
    split_at = per_group * head_width
    query = summed[:, :split_at].reshape(rows_here, per_group, head_width)
    query = rotate(rms_scale(query, qk_gains[0]), position).astype(jnp.bfloat16)
    key_part = summed[:, split_at : split_at + head_width][:, None, :]
    key_new = rotate(rms_scale(key_part, qk_gains[1]), position)[:, 0].astype(jnp.bfloat16)
    value_new = rms_scale(summed[:, split_at + head_width :], 1.0).astype(jnp.bfloat16)

    slot_base = (req_position * hid_total + hid_position) * pool_size
    local = my_tables - slot_base
    slots = jnp.arange(pool_size, dtype=jnp.int32)
    match = local[:, :, None] == slots[None, None, :]
    page_ids = jnp.arange(my_tables.shape[1], dtype=jnp.int32)
    owner_hit = jnp.any(match, axis=1)
    page_of = jnp.sum(jnp.where(match, page_ids[None, :, None], 0), axis=(0, 1))
    cache_pos = page_of[:, None] * page_size + jnp.arange(page_size, dtype=jnp.int32)[None, :]
    live = owner_hit[:, :, None] & (cache_pos[None] < my_lengths[:, None, None])
    live = live.reshape(rows_here, 1, pool_size * page_size)

    cached_keys = kv_cache[:, 0].reshape(pool_size * page_size, head_width)
    cached_values = kv_cache[:, 1].reshape(pool_size * page_size, head_width)
    scale_factor = head_width ** (-0.5)
    scores = jnp.dot(
        query.reshape(rows_here * per_group, head_width),
        cached_keys.T,
        preferred_element_type=jnp.float32,
    ).reshape(rows_here, per_group, -1) * scale_factor
    masked = jnp.where(live, scores, neg_large)
    highest_cached = jnp.max(masked, axis=2)
    weights = jnp.where(live, jnp.exp(masked - highest_cached[..., None]), 0.0)
    totals = jnp.sum(weights, axis=2)
    weighted = jnp.dot(
        weights.astype(jnp.bfloat16).reshape(rows_here * per_group, -1),
        cached_values,
        preferred_element_type=jnp.float32,
    ).reshape(rows_here, per_group, head_width)
    query_f = query.astype(jnp.float32)
    own_score = jnp.sum(query_f * key_new.astype(jnp.float32)[:, None, :], axis=-1) * scale_factor
    highest = jnp.maximum(highest_cached, own_score)
    old_scale = jnp.exp(highest_cached - highest)
    new_scale = jnp.exp(own_score - highest)
    combined = (
        weighted * old_scale[..., None]
        + new_scale[..., None] * value_new.astype(jnp.float32)[:, None, :]
    ) / (totals * old_scale + new_scale)[..., None]
    attended = combined.astype(jnp.bfloat16).reshape(rows_here, per_group * head_width)

    slice_width = output_weight.shape[1]
    send_att = attended.reshape(rows_here, req_total, slice_width).transpose(1, 0, 2)
    got_att = exchange(send_att, ("req",), 2).reshape(request_count, slice_width)
    att_natural = jnp.dot(order_b.T, got_att, preferred_element_type=jnp.float32).astype(
        jnp.bfloat16
    )
    proj_partial = jnp.dot(att_natural, output_weight[0], preferred_element_type=jnp.float32)
    proj_partial = proj_partial.astype(jnp.bfloat16).reshape(
        req_total * kv_total, half_rows, model_width
    )
    projected = jnp.sum(
        exchange(proj_partial, ("req", "kv"), 3).astype(jnp.float32), axis=0
    )

    residual = lax.dynamic_slice_in_dim(own_rows, kv_position * half_rows, half_rows, 0)
    middle = (residual + rms_scale(projected, gains[1])).astype(jnp.bfloat16)
    ffn_input = rms_scale(middle.astype(jnp.float32), gains[2]).astype(jnp.bfloat16)
    ffn_rows = exchange(ffn_input, ("kv", "hid"), 4, bcast=True).reshape(-1, model_width)
    gate_up = jnp.einsum(
        "nd,dgf->ngf", ffn_rows, w_gateup, preferred_element_type=jnp.float32
    )
    hidden = (jax.nn.gelu(gate_up[:, 0], approximate=True) * gate_up[:, 1]).astype(jnp.bfloat16)
    ffn_partial = jnp.dot(hidden, w_down, preferred_element_type=jnp.float32).astype(
        jnp.bfloat16
    )
    ffn_partial = ffn_partial.reshape(kv_total * hid_total, half_rows, model_width)
    ffn_sum = jnp.sum(exchange(ffn_partial, ("kv", "hid"), 5).astype(jnp.float32), axis=0)
    result = (middle.astype(jnp.float32) + rms_scale(ffn_sum, gains[3])).astype(jnp.bfloat16)
    return result[:, None, :]


def solution(mesh):
    return jax.shard_map(
        shards,
        mesh=mesh,
        in_specs=(
            P("req", "hid", None),
            P(),
            P(),
            P("req", "kv"),
            P("req", None, "kv"),
            P("kv", "req", None),
            P(None, None, ("kv", "hid")),
            P(("kv", "hid"), None),
            P(("req", "hid"), None, None, "kv"),
            P(),
            P(),
        ),
        out_specs=P(("req", "kv"), "hid", None),
        check_vma=False,
    )
```

```python
import functools

import jax
import jax.numpy as jnp
from jax import lax
from jax.experimental import pallas as pl
from jax.experimental.pallas import tpu as pltpu
from jax.sharding import PartitionSpec as P

eps_norm = 1e-06
rope_base = 1000000.0
neg_large = -1e30
MESH = pl.DeviceIdType.MESH
AXES = ("req", "kv", "hid")


def group_layout(group):
    sizes = [lax.axis_size(a) for a in group]
    me = 0
    for a, s in zip(group, sizes):
        me = me * s + lax.axis_index(a)
    total = 1
    for s in sizes:
        total *= s
    return sizes, me, total


def device_of(group, sizes, position):
    coords = {a: lax.axis_index(a) for a in AXES}
    rest = position
    for a, s in reversed(list(zip(group, sizes))):
        coords[a] = rest % s
        rest = rest // s
    return tuple(coords[a] for a in AXES)


def exchange_kernel(group, bcast, x_ref, y_ref, send_sem, recv_sem):
    sizes, me, n = group_layout(group)
    barrier = pltpu.get_barrier_semaphore()
    for s in range(1, n):
        peer = lax.rem(me + s, n)
        pl.semaphore_signal(
            barrier, inc=1, device_id=device_of(group, sizes, peer), device_id_type=MESH
        )
    pl.semaphore_wait(barrier, n - 1)
    copies = []
    for s in range(1, n):
        peer = lax.rem(me + s, n)
        src = x_ref if bcast else x_ref.at[peer]
        copy = pltpu.make_async_remote_copy(
            src_ref=src,
            dst_ref=y_ref.at[me],
            send_sem=send_sem.at[s],
            recv_sem=recv_sem.at[s],
            device_id=device_of(group, sizes, peer),
            device_id_type=MESH,
        )
        copy.start()
        copies.append(copy)
    if bcast:
        y_ref[me] = x_ref[...]
    else:
        y_ref[me] = x_ref[me]
    for s in range(1, n):
        copies[s - 1].wait_send()
        origin = lax.rem(me + n - s, n)
        src = x_ref if bcast else x_ref.at[origin]
        pltpu.make_async_remote_copy(
            src_ref=src,
            dst_ref=y_ref.at[origin],
            send_sem=send_sem.at[s],
            recv_sem=recv_sem.at[s],
            device_id=device_of(group, sizes, origin),
            device_id_type=MESH,
        ).wait_recv()


def exchange(x, group, cid, bcast=False):
    n = 1
    for a in group:
        n *= lax.axis_size(a)
    block = x.shape if bcast else x.shape[1:]
    return pl.pallas_call(
        functools.partial(exchange_kernel, group, bcast),
        out_shape=jax.ShapeDtypeStruct((n,) + tuple(block), x.dtype),
        in_specs=[pl.BlockSpec(memory_space=pltpu.VMEM)],
        out_specs=pl.BlockSpec(memory_space=pltpu.VMEM),
        scratch_shapes=[pltpu.SemaphoreType.DMA((n,)), pltpu.SemaphoreType.DMA((n,))],
        compiler_params=pltpu.CompilerParams(collective_id=cid, has_side_effects=True),
    )(x)


def rms_scale(value_entries, gain_row):
    mean_square = jnp.mean(value_entries * value_entries, axis=-1, keepdims=True)
    return value_entries * lax.rsqrt(mean_square + eps_norm) * gain_row


def rotate(value_entries, position):
    half_width = value_entries.shape[-1] // 2
    frequency = rope_base ** (
        -jnp.arange(half_width, dtype=jnp.float32) * 2.0 / value_entries.shape[-1]
    )
    angles = position[:, None, None] * frequency
    cosines = jnp.cos(angles)
    sines = jnp.sin(angles)
    first_half = value_entries[..., :half_width]
    second_half = value_entries[..., half_width:]
    return jnp.concatenate(
        [first_half * cosines - second_half * sines, second_half * cosines + first_half * sines],
        axis=-1,
    )


def shards(
    tokens,
    gains,
    qk_gains,
    w_query,
    key_value_weight,
    output_weight,
    w_gateup,
    w_down,
    kv_cache,
    lengths,
    page_table,
):
    req_position = lax.axis_index("req")
    kv_position = lax.axis_index("kv")
    hid_position = lax.axis_index("hid")
    req_total = lax.axis_size("req")
    hid_total = lax.axis_size("hid")
    kv_total = lax.axis_size("kv")
    rows_here, _, model_width = tokens.shape
    half_rows = rows_here // kv_total
    head_width = qk_gains.shape[1]
    per_group = w_query.shape[1] // head_width
    pool_size, _, page_size, _ = kv_cache.shape
    request_count = rows_here * req_total
    feature_width = w_query.shape[0]

    own_rows = tokens[:, 0, :].astype(jnp.float32)
    normed = rms_scale(own_rows, gains[0]).astype(jnp.bfloat16)

    send_tokens = normed.reshape(rows_here, req_total, feature_width).transpose(1, 0, 2)
    columns = exchange(send_tokens, ("req",), 0).reshape(request_count, feature_width)

    group_lengths = lax.dynamic_index_in_dim(lengths, hid_position, axis=1, keepdims=False)
    group_table = lax.dynamic_index_in_dim(page_table, hid_position, axis=1, keepdims=False)
    request_ids = jnp.arange(request_count, dtype=jnp.int32)
    pool_of = (group_table[:, 0] // pool_size) // hid_total
    pool_pos = pool_of * rows_here + request_ids % rows_here
    order = pool_pos[None, :] == request_ids[:, None]
    order_b = order.astype(jnp.bfloat16)
    columns_pooled = jnp.dot(order_b, columns, preferred_element_type=jnp.float32).astype(
        jnp.bfloat16
    )

    projection = jnp.concatenate(
        [w_query, key_value_weight.reshape(key_value_weight.shape[0], -1)], axis=1
    )
    partial = jnp.dot(columns_pooled, projection, preferred_element_type=jnp.float32)
    qkv_width = partial.shape[1]
    gathered = exchange(partial.reshape(req_total, 8, -1), ("req",), 1)
    summed = jnp.sum(gathered.reshape(req_total, rows_here, qkv_width), axis=0)

    mine = lax.dynamic_slice_in_dim(order, req_position * rows_here, rows_here, 0)
    my_lengths = jnp.sum(jnp.where(mine, group_lengths[None, :], 0), axis=1)
    my_tables = jnp.sum(jnp.where(mine[:, :, None], group_table[None, :, :], 0), axis=1)

    position = my_lengths.astype(jnp.float32)
    split_at = per_group * head_width
    query = summed[:, :split_at].reshape(rows_here, per_group, head_width)
    query = rotate(rms_scale(query, qk_gains[0]), position).astype(jnp.bfloat16)
    key_part = summed[:, split_at : split_at + head_width][:, None, :]
    key_new = rotate(rms_scale(key_part, qk_gains[1]), position)[:, 0].astype(jnp.bfloat16)
    value_new = rms_scale(summed[:, split_at + head_width :], 1.0).astype(jnp.bfloat16)

    slot_base = (req_position * hid_total + hid_position) * pool_size
    local = my_tables - slot_base
    slots = jnp.arange(pool_size, dtype=jnp.int32)
    match = local[:, :, None] == slots[None, None, :]
    page_ids = jnp.arange(my_tables.shape[1], dtype=jnp.int32)
    owner_hit = jnp.any(match, axis=1)
    page_of = jnp.sum(jnp.where(match, page_ids[None, :, None], 0), axis=(0, 1))
    cache_pos = page_of[:, None] * page_size + jnp.arange(page_size, dtype=jnp.int32)[None, :]
    live = owner_hit[:, :, None] & (cache_pos[None] < my_lengths[:, None, None])
    live = live.reshape(rows_here, 1, pool_size * page_size)

    cached_keys = kv_cache[:, 0].reshape(pool_size * page_size, head_width)
    cached_values = kv_cache[:, 1].reshape(pool_size * page_size, head_width)
    scale_factor = head_width ** (-0.5)
    scores = jnp.dot(
        query.reshape(rows_here * per_group, head_width),
        cached_keys.T,
        preferred_element_type=jnp.float32,
    ).reshape(rows_here, per_group, -1) * scale_factor
    masked = jnp.where(live, scores, neg_large)
    highest_cached = jnp.max(masked, axis=2)
    weights = jnp.where(live, jnp.exp(masked - highest_cached[..., None]), 0.0)
    totals = jnp.sum(weights, axis=2)
    weighted = jnp.dot(
        weights.astype(jnp.bfloat16).reshape(rows_here * per_group, -1),
        cached_values,
        preferred_element_type=jnp.float32,
    ).reshape(rows_here, per_group, head_width)
    query_f = query.astype(jnp.float32)
    own_score = jnp.sum(query_f * key_new.astype(jnp.float32)[:, None, :], axis=-1) * scale_factor
    highest = jnp.maximum(highest_cached, own_score)
    old_scale = jnp.exp(highest_cached - highest)
    new_scale = jnp.exp(own_score - highest)
    combined = (
        weighted * old_scale[..., None]
        + new_scale[..., None] * value_new.astype(jnp.float32)[:, None, :]
    ) / (totals * old_scale + new_scale)[..., None]
    attended = combined.astype(jnp.bfloat16).reshape(rows_here, per_group * head_width)

    slice_width = output_weight.shape[1]
    send_att = attended.reshape(rows_here, req_total, slice_width).transpose(1, 0, 2)
    got_att = exchange(send_att, ("req",), 2).reshape(request_count, slice_width)
    att_natural = jnp.dot(order_b.T, got_att, preferred_element_type=jnp.float32).astype(
        jnp.bfloat16
    )
    proj_partial = jnp.dot(att_natural, output_weight[0], preferred_element_type=jnp.float32)
    proj_partial = proj_partial.astype(jnp.bfloat16).reshape(req_total * kv_total, 16, -1)
    projected = jnp.sum(
        exchange(proj_partial, ("req", "kv"), 3)
        .reshape(req_total * kv_total, half_rows, model_width)
        .astype(jnp.float32),
        axis=0,
    )

    residual = lax.dynamic_slice_in_dim(own_rows, kv_position * half_rows, half_rows, 0)
    middle = (residual + rms_scale(projected, gains[1])).astype(jnp.bfloat16)
    ffn_input = rms_scale(middle.astype(jnp.float32), gains[2]).astype(jnp.bfloat16)
    ffn_rows = exchange(ffn_input.reshape(16, -1), ("kv", "hid"), 4, bcast=True).reshape(
        -1, model_width
    )
    gate_up = jnp.einsum(
        "nd,dgf->ngf", ffn_rows, w_gateup, preferred_element_type=jnp.float32
    )
    hidden = (jax.nn.gelu(gate_up[:, 0], approximate=True) * gate_up[:, 1]).astype(jnp.bfloat16)
    ffn_partial = jnp.dot(hidden, w_down, preferred_element_type=jnp.float32).astype(
        jnp.bfloat16
    )
    ffn_partial = ffn_partial.reshape(kv_total * hid_total, 16, -1)
    ffn_sum = jnp.sum(
        exchange(ffn_partial, ("kv", "hid"), 5)
        .reshape(kv_total * hid_total, half_rows, model_width)
        .astype(jnp.float32),
        axis=0,
    )
    result = (middle.astype(jnp.float32) + rms_scale(ffn_sum, gains[3])).astype(jnp.bfloat16)
    return result[:, None, :]


def solution(mesh):
    return jax.shard_map(
        shards,
        mesh=mesh,
        in_specs=(
            P("req", "hid", None),
            P(),
            P(),
            P("req", "kv"),
            P("req", None, "kv"),
            P("kv", "req", None),
            P(None, None, ("kv", "hid")),
            P(("kv", "hid"), None),
            P(("req", "hid"), None, None, "kv"),
            P(),
            P(),
        ),
        out_specs=P(("req", "kv"), "hid", None),
        check_vma=False,
    )
```

```python
import functools

import jax
import jax.numpy as jnp
from jax import lax
from jax.experimental import pallas as pl
from jax.experimental.pallas import tpu as pltpu
from jax.sharding import PartitionSpec as P

eps_norm = 1e-06
rope_base = 1000000.0
neg_large = -1e30
MESH = pl.DeviceIdType.MESH
AXES = ("req", "kv", "hid")


def group_layout(group):
    sizes = [lax.axis_size(a) for a in group]
    me = 0
    for a, s in zip(group, sizes):
        me = me * s + lax.axis_index(a)
    total = 1
    for s in sizes:
        total *= s
    return sizes, me, total


def device_of(group, sizes, position):
    coords = {a: lax.axis_index(a) for a in AXES}
    rest = position
    for a, s in reversed(list(zip(group, sizes))):
        coords[a] = rest % s
        rest = rest // s
    return tuple(coords[a] for a in AXES)


def exchange_kernel(group, bcast, x_ref, y_ref, send_sem, recv_sem):
    sizes, me, n = group_layout(group)
    barrier = pltpu.get_barrier_semaphore()
    for s in range(1, n):
        peer = lax.rem(me + s, n)
        pl.semaphore_signal(
            barrier, inc=1, device_id=device_of(group, sizes, peer), device_id_type=MESH
        )
    pl.semaphore_wait(barrier, n - 1)
    copies = []
    for s in range(1, n):
        peer = lax.rem(me + s, n)
        src = x_ref if bcast else x_ref.at[peer]
        copy = pltpu.make_async_remote_copy(
            src_ref=src,
            dst_ref=y_ref.at[me],
            send_sem=send_sem.at[s],
            recv_sem=recv_sem.at[s],
            device_id=device_of(group, sizes, peer),
            device_id_type=MESH,
        )
        copy.start()
        copies.append(copy)
    if bcast:
        y_ref[me] = x_ref[...]
    else:
        y_ref[me] = x_ref[me]
    for s in range(1, n):
        copies[s - 1].wait_send()
        origin = lax.rem(me + n - s, n)
        src = x_ref if bcast else x_ref.at[origin]
        pltpu.make_async_remote_copy(
            src_ref=src,
            dst_ref=y_ref.at[origin],
            send_sem=send_sem.at[s],
            recv_sem=recv_sem.at[s],
            device_id=device_of(group, sizes, origin),
            device_id_type=MESH,
        ).wait_recv()


def exchange(x, group, cid, bcast=False):
    n = 1
    for a in group:
        n *= lax.axis_size(a)
    block = x.shape if bcast else x.shape[1:]
    return pl.pallas_call(
        functools.partial(exchange_kernel, group, bcast),
        out_shape=jax.ShapeDtypeStruct((n,) + tuple(block), x.dtype),
        in_specs=[pl.BlockSpec(memory_space=pltpu.VMEM)],
        out_specs=pl.BlockSpec(memory_space=pltpu.VMEM),
        scratch_shapes=[pltpu.SemaphoreType.DMA((n,)), pltpu.SemaphoreType.DMA((n,))],
        compiler_params=pltpu.CompilerParams(collective_id=cid, has_side_effects=True),
    )(x)


def start_copies(group, src_of, dst_ref, send_sem, recv_sem):
    sizes, me, n = group_layout(group)
    copies = []
    for s in range(1, n):
        peer = lax.rem(me + s, n)
        copy = pltpu.make_async_remote_copy(
            src_ref=src_of(peer),
            dst_ref=dst_ref.at[me],
            send_sem=send_sem.at[s],
            recv_sem=recv_sem.at[s],
            device_id=device_of(group, sizes, peer),
            device_id_type=MESH,
        )
        copy.start()
        copies.append(copy)

    def finish():
        for s in range(1, n):
            copies[s - 1].wait_send()
            origin = lax.rem(me + n - s, n)
            pltpu.make_async_remote_copy(
                src_ref=src_of(origin),
                dst_ref=dst_ref.at[origin],
                send_sem=send_sem.at[s],
                recv_sem=recv_sem.at[s],
                device_id=device_of(group, sizes, origin),
                device_id_type=MESH,
            ).wait_recv()

    return me, finish


def rms_rows(value_entries, gain_row):
    mean_square = jnp.mean(value_entries * value_entries, axis=-1, keepdims=True)
    return value_entries * lax.rsqrt(mean_square + eps_norm) * gain_row


def tail_kernel(
    att_ref, unperm_ref, wout_ref, resid_ref, gains_ref, wgu_hbm, wd_hbm,
    out_ref,
    y_att, att_rows, w_pad, send_proj, y_proj, ffn_src, y_ffn, ffn_rows, ffn_out,
    send_red, y_red, wgu_v, wd_v,
    att_send, att_recv, proj_send, proj_recv, ffn_send, ffn_recv, red_send, red_recv, w_sem,
):
    wgu_copy = pltpu.make_async_copy(wgu_hbm, wgu_v, w_sem.at[0])
    wd_copy = pltpu.make_async_copy(wd_hbm, wd_v, w_sem.at[1])
    wgu_copy.start()
    wd_copy.start()

    wide = ("req", "kv")
    narrow = ("kv", "hid")
    wide_sizes, wide_me, wide_n = group_layout(wide)
    narrow_sizes, narrow_me, narrow_n = group_layout(narrow)
    half = narrow_n // 2
    barrier = pltpu.get_barrier_semaphore()
    for s in range(1, wide_n):
        peer = lax.rem(wide_me + s, wide_n)
        pl.semaphore_signal(
            barrier, inc=1, device_id=device_of(wide, wide_sizes, peer), device_id_type=MESH
        )
    for s in range(1, narrow_n):
        if s == half:
            continue
        peer = lax.rem(narrow_me + s, narrow_n)
        pl.semaphore_signal(
            barrier, inc=1, device_id=device_of(narrow, narrow_sizes, peer), device_id_type=MESH
        )
    pl.semaphore_wait(barrier, wide_n - 1 + narrow_n - 2)

    att_me, att_finish = start_copies(("req",), lambda k: att_ref.at[k], y_att, att_send, att_recv)
    y_att[att_me] = att_ref[att_me]
    att_rows[...] = jnp.zeros_like(att_rows)
    w_pad[...] = jnp.zeros_like(w_pad)
    rows_w = wout_ref.shape[0]
    w_pad[0:rows_w, :] = wout_ref[...]
    att_finish()
    n_req, per_pool, slice_width = y_att.shape
    for k in range(n_req):
        att_rows[8 * k : 8 * k + per_pool, 0:slice_width] = y_att[k].astype(jnp.float32)
    att_nat = jnp.dot(
        unperm_ref[...], att_rows[...].astype(jnp.bfloat16), preferred_element_type=jnp.float32
    ).astype(jnp.bfloat16)
    proj = jnp.dot(att_nat, w_pad[...], preferred_element_type=jnp.float32)
    n_wide, owned, width = send_proj.shape
    for q in range(n_wide):
        send_proj[q] = proj[owned * q : owned * (q + 1)].astype(jnp.bfloat16)

    proj_me, proj_finish = start_copies(wide, lambda k: send_proj.at[k], y_proj, proj_send, proj_recv)
    y_proj[proj_me] = send_proj[proj_me]
    proj_finish()
    projected = y_proj[0].astype(jnp.float32)
    for k in range(1, n_wide):
        projected = projected + y_proj[k].astype(jnp.float32)
    middle = (resid_ref[...] + rms_rows(projected, gains_ref[1:2, :])).astype(jnp.bfloat16)
    ffn_src[...] = rms_rows(middle.astype(jnp.float32), gains_ref[2:3, :]).astype(jnp.bfloat16)

    ffn_me, ffn_finish = start_copies(narrow, lambda k: ffn_src, y_ffn, ffn_send, ffn_recv)
    y_ffn[ffn_me] = ffn_src[...]
    ffn_finish()
    for k in range(narrow_n):
        ffn_rows[owned * k : owned * (k + 1), :] = y_ffn[k].astype(jnp.float32)
    wgu_copy.wait()
    wd_copy.wait()
    gate_up = jnp.dot(
        ffn_rows[...].astype(jnp.bfloat16), wgu_v[...], preferred_element_type=jnp.float32
    )
    hidden_width = wd_v.shape[0]
    hidden = (
        jax.nn.gelu(gate_up[:, :hidden_width], approximate=True) * gate_up[:, hidden_width:]
    ).astype(jnp.bfloat16)
    ffn_out[...] = jnp.dot(hidden, wd_v[...], preferred_element_type=jnp.float32)
    for k in range(narrow_n):
        send_red[k] = ffn_out[owned * k : owned * (k + 1), :].astype(jnp.bfloat16)

    red_me, red_finish = start_copies(narrow, lambda k: send_red.at[k], y_red, red_send, red_recv)
    y_red[red_me] = send_red[red_me]
    red_finish()
    ffn_sum = y_red[0].astype(jnp.float32)
    for k in range(1, narrow_n):
        ffn_sum = ffn_sum + y_red[k].astype(jnp.float32)
    out_ref[...] = (middle.astype(jnp.float32) + rms_rows(ffn_sum, gains_ref[3:4, :])).astype(
        out_ref.dtype
    )


def tail(send_att, unperm, wout, residual, gains, wgu, wd, cid):
    n_req = lax.axis_size("req")
    n_wide = n_req * lax.axis_size("kv")
    n_narrow = lax.axis_size("kv") * lax.axis_size("hid")
    owned, width = residual.shape
    vmem = pl.BlockSpec(memory_space=pltpu.VMEM)
    anywhere = pl.BlockSpec(memory_space=pl.ANY)
    dma = pltpu.SemaphoreType.DMA
    return pl.pallas_call(
        tail_kernel,
        out_shape=jax.ShapeDtypeStruct((owned, width), jnp.bfloat16),
        in_specs=[vmem, vmem, vmem, vmem, vmem, anywhere, anywhere],
        out_specs=vmem,
        scratch_shapes=[
            pltpu.VMEM(send_att.shape, jnp.bfloat16),
            pltpu.VMEM((8 * n_req, 128), jnp.float32),
            pltpu.VMEM((128, width), jnp.bfloat16),
            pltpu.VMEM((n_wide, owned, width), jnp.bfloat16),
            pltpu.VMEM((n_wide, owned, width), jnp.bfloat16),
            pltpu.VMEM((owned, width), jnp.bfloat16),
            pltpu.VMEM((n_narrow, owned, width), jnp.bfloat16),
            pltpu.VMEM((n_narrow * owned, width), jnp.float32),
            pltpu.VMEM((n_narrow * owned, width), jnp.float32),
            pltpu.VMEM((n_narrow, owned, width), jnp.bfloat16),
            pltpu.VMEM((n_narrow, owned, width), jnp.bfloat16),
            pltpu.VMEM(wgu.shape, jnp.bfloat16),
            pltpu.VMEM(wd.shape, jnp.bfloat16),
            dma((n_req,)), dma((n_req,)),
            dma((n_wide,)), dma((n_wide,)),
            dma((n_narrow,)), dma((n_narrow,)),
            dma((n_narrow,)), dma((n_narrow,)),
            dma((2,)),
        ],
        compiler_params=pltpu.CompilerParams(
            collective_id=cid, has_side_effects=True, vmem_limit_bytes=48 * 1024 * 1024
        ),
    )(send_att, unperm, wout, residual, gains, wgu, wd)


def rms_scale(value_entries, gain_row):
    mean_square = jnp.mean(value_entries * value_entries, axis=-1, keepdims=True)
    return value_entries * lax.rsqrt(mean_square + eps_norm) * gain_row


def rotate(value_entries, position):
    half_width = value_entries.shape[-1] // 2
    frequency = rope_base ** (
        -jnp.arange(half_width, dtype=jnp.float32) * 2.0 / value_entries.shape[-1]
    )
    angles = position[:, None, None] * frequency
    cosines = jnp.cos(angles)
    sines = jnp.sin(angles)
    first_half = value_entries[..., :half_width]
    second_half = value_entries[..., half_width:]
    return jnp.concatenate(
        [first_half * cosines - second_half * sines, second_half * cosines + first_half * sines],
        axis=-1,
    )


def shards(
    tokens,
    gains,
    qk_gains,
    w_query,
    key_value_weight,
    output_weight,
    w_gateup,
    w_down,
    kv_cache,
    lengths,
    page_table,
):
    req_position = lax.axis_index("req")
    kv_position = lax.axis_index("kv")
    hid_position = lax.axis_index("hid")
    req_total = lax.axis_size("req")
    hid_total = lax.axis_size("hid")
    kv_total = lax.axis_size("kv")
    rows_here, _, model_width = tokens.shape
    half_rows = rows_here // kv_total
    head_width = qk_gains.shape[1]
    per_group = w_query.shape[1] // head_width
    pool_size, _, page_size, _ = kv_cache.shape
    request_count = rows_here * req_total
    feature_width = w_query.shape[0]

    own_rows = tokens[:, 0, :].astype(jnp.float32)
    normed = rms_scale(own_rows, gains[0]).astype(jnp.bfloat16)

    send_tokens = normed.reshape(rows_here, req_total, feature_width).transpose(1, 0, 2)
    columns = exchange(send_tokens, ("req",), 0).reshape(request_count, feature_width)

    group_lengths = lax.dynamic_index_in_dim(lengths, hid_position, axis=1, keepdims=False)
    group_table = lax.dynamic_index_in_dim(page_table, hid_position, axis=1, keepdims=False)
    request_ids = jnp.arange(request_count, dtype=jnp.int32)
    pool_of = (group_table[:, 0] // pool_size) // hid_total
    pool_pos = pool_of * rows_here + request_ids % rows_here
    order = pool_pos[None, :] == request_ids[:, None]
    order_b = order.astype(jnp.bfloat16)
    columns_pooled = jnp.dot(order_b, columns, preferred_element_type=jnp.float32).astype(
        jnp.bfloat16
    )

    projection = jnp.concatenate(
        [w_query, key_value_weight.reshape(key_value_weight.shape[0], -1)], axis=1
    )
    partial = jnp.dot(columns_pooled, projection, preferred_element_type=jnp.float32)
    gathered = exchange(partial.reshape(req_total, rows_here, -1), ("req",), 1)
    summed = jnp.sum(gathered, axis=0)

    mine = lax.dynamic_slice_in_dim(order, req_position * rows_here, rows_here, 0)
    my_lengths = jnp.sum(jnp.where(mine, group_lengths[None, :], 0), axis=1)
    my_tables = jnp.sum(jnp.where(mine[:, :, None], group_table[None, :, :], 0), axis=1)

    position = my_lengths.astype(jnp.float32)
    split_at = per_group * head_width
    query = summed[:, :split_at].reshape(rows_here, per_group, head_width)
    query = rotate(rms_scale(query, qk_gains[0]), position).astype(jnp.bfloat16)
    key_part = summed[:, split_at : split_at + head_width][:, None, :]
    key_new = rotate(rms_scale(key_part, qk_gains[1]), position)[:, 0].astype(jnp.bfloat16)
    value_new = rms_scale(summed[:, split_at + head_width :], 1.0).astype(jnp.bfloat16)

    slot_base = (req_position * hid_total + hid_position) * pool_size
    local = my_tables - slot_base
    slots = jnp.arange(pool_size, dtype=jnp.int32)
    match = local[:, :, None] == slots[None, None, :]
    page_ids = jnp.arange(my_tables.shape[1], dtype=jnp.int32)
    owner_hit = jnp.any(match, axis=1)
    page_of = jnp.sum(jnp.where(match, page_ids[None, :, None], 0), axis=(0, 1))
    cache_pos = page_of[:, None] * page_size + jnp.arange(page_size, dtype=jnp.int32)[None, :]
    live = owner_hit[:, :, None] & (cache_pos[None] < my_lengths[:, None, None])
    live = live.reshape(rows_here, 1, pool_size * page_size)

    cached_keys = kv_cache[:, 0].reshape(pool_size * page_size, head_width)
    cached_values = kv_cache[:, 1].reshape(pool_size * page_size, head_width)
    scale_factor = head_width ** (-0.5)
    scores = jnp.dot(
        query.reshape(rows_here * per_group, head_width),
        cached_keys.T,
        preferred_element_type=jnp.float32,
    ).reshape(rows_here, per_group, -1) * scale_factor
    masked = jnp.where(live, scores, neg_large)
    highest_cached = jnp.max(masked, axis=2)
    weights = jnp.where(live, jnp.exp(masked - highest_cached[..., None]), 0.0)
    totals = jnp.sum(weights, axis=2)
    weighted = jnp.dot(
        weights.astype(jnp.bfloat16).reshape(rows_here * per_group, -1),
        cached_values,
        preferred_element_type=jnp.float32,
    ).reshape(rows_here, per_group, head_width)
    query_f = query.astype(jnp.float32)
    own_score = jnp.sum(query_f * key_new.astype(jnp.float32)[:, None, :], axis=-1) * scale_factor
    highest = jnp.maximum(highest_cached, own_score)
    old_scale = jnp.exp(highest_cached - highest)
    new_scale = jnp.exp(own_score - highest)
    combined = (
        weighted * old_scale[..., None]
        + new_scale[..., None] * value_new.astype(jnp.float32)[:, None, :]
    ) / (totals * old_scale + new_scale)[..., None]
    attended = combined.astype(jnp.bfloat16).reshape(rows_here, per_group * head_width)

    slice_width = output_weight.shape[1]
    send_att = attended.reshape(rows_here, req_total, slice_width).transpose(1, 0, 2)
    unperm = order.T.reshape(request_count, req_total, rows_here)
    unperm = jnp.pad(unperm, ((0, 0), (0, 0), (0, 8 - rows_here)))
    unperm = unperm.reshape(request_count, 8 * req_total).astype(jnp.bfloat16)
    residual = lax.dynamic_slice_in_dim(own_rows, kv_position * half_rows, half_rows, 0)
    hidden_width = w_down.shape[0]
    result = tail(
        send_att,
        unperm,
        output_weight[0],
        residual,
        gains,
        w_gateup.reshape(model_width, 2 * hidden_width),
        w_down,
        2,
    )
    return result[:, None, :]


def solution(mesh):
    return jax.shard_map(
        shards,
        mesh=mesh,
        in_specs=(
            P("req", "hid", None),
            P(),
            P(),
            P("req", "kv"),
            P("req", None, "kv"),
            P("kv", "req", None),
            P(None, None, ("kv", "hid")),
            P(("kv", "hid"), None),
            P(("req", "hid"), None, None, "kv"),
            P(),
            P(),
        ),
        out_specs=P(("req", "kv"), "hid", None),
        check_vma=False,
    )
```

```python
import functools

import jax
import jax.numpy as jnp
from jax import lax
from jax.experimental import pallas as pl
from jax.experimental.pallas import tpu as pltpu
from jax.sharding import PartitionSpec as P

eps_norm = 1e-06
rope_base = 1000000.0
neg_large = -1e30
MESH = pl.DeviceIdType.MESH
AXES = ("req", "kv", "hid")


def group_layout(group):
    sizes = [lax.axis_size(a) for a in group]
    me = 0
    for a, s in zip(group, sizes):
        me = me * s + lax.axis_index(a)
    total = 1
    for s in sizes:
        total *= s
    return sizes, me, total


def device_of(group, sizes, position):
    coords = {a: lax.axis_index(a) for a in AXES}
    rest = position
    for a, s in reversed(list(zip(group, sizes))):
        coords[a] = rest % s
        rest = rest // s
    return tuple(coords[a] for a in AXES)


def exchange_kernel(group, bcast, x_ref, y_ref, send_sem, recv_sem):
    sizes, me, n = group_layout(group)
    barrier = pltpu.get_barrier_semaphore()
    for s in range(1, n):
        peer = lax.rem(me + s, n)
        pl.semaphore_signal(
            barrier, inc=1, device_id=device_of(group, sizes, peer), device_id_type=MESH
        )
    pl.semaphore_wait(barrier, n - 1)
    copies = []
    for s in range(1, n):
        peer = lax.rem(me + s, n)
        src = x_ref if bcast else x_ref.at[peer]
        copy = pltpu.make_async_remote_copy(
            src_ref=src,
            dst_ref=y_ref.at[me],
            send_sem=send_sem.at[s],
            recv_sem=recv_sem.at[s],
            device_id=device_of(group, sizes, peer),
            device_id_type=MESH,
        )
        copy.start()
        copies.append(copy)
    if bcast:
        y_ref[me] = x_ref[...]
    else:
        y_ref[me] = x_ref[me]
    for s in range(1, n):
        copies[s - 1].wait_send()
        origin = lax.rem(me + n - s, n)
        src = x_ref if bcast else x_ref.at[origin]
        pltpu.make_async_remote_copy(
            src_ref=src,
            dst_ref=y_ref.at[origin],
            send_sem=send_sem.at[s],
            recv_sem=recv_sem.at[s],
            device_id=device_of(group, sizes, origin),
            device_id_type=MESH,
        ).wait_recv()


def exchange(x, group, cid, bcast=False):
    n = 1
    for a in group:
        n *= lax.axis_size(a)
    block = x.shape if bcast else x.shape[1:]
    return pl.pallas_call(
        functools.partial(exchange_kernel, group, bcast),
        out_shape=jax.ShapeDtypeStruct((n,) + tuple(block), x.dtype),
        in_specs=[pl.BlockSpec(memory_space=pltpu.VMEM)],
        out_specs=pl.BlockSpec(memory_space=pltpu.VMEM),
        scratch_shapes=[pltpu.SemaphoreType.DMA((n,)), pltpu.SemaphoreType.DMA((n,))],
        compiler_params=pltpu.CompilerParams(collective_id=cid, has_side_effects=True),
    )(x)


def start_copies(group, src_of, dst_ref, send_sem, recv_sem):
    sizes, me, n = group_layout(group)
    copies = []
    for s in range(1, n):
        peer = lax.rem(me + s, n)
        copy = pltpu.make_async_remote_copy(
            src_ref=src_of(peer),
            dst_ref=dst_ref.at[me],
            send_sem=send_sem.at[s],
            recv_sem=recv_sem.at[s],
            device_id=device_of(group, sizes, peer),
            device_id_type=MESH,
        )
        copy.start()
        copies.append(copy)

    def finish():
        for s in range(1, n):
            copies[s - 1].wait_send()
            origin = lax.rem(me + n - s, n)
            pltpu.make_async_remote_copy(
                src_ref=src_of(origin),
                dst_ref=dst_ref.at[origin],
                send_sem=send_sem.at[s],
                recv_sem=recv_sem.at[s],
                device_id=device_of(group, sizes, origin),
                device_id_type=MESH,
            ).wait_recv()

    return me, finish


def rms_rows(value_entries, gain_row):
    mean_square = jnp.mean(value_entries * value_entries, axis=-1, keepdims=True)
    return value_entries * lax.rsqrt(mean_square + eps_norm) * gain_row


def layer_kernel(
    tok_ref, gains_ref, qkg_ref, order_ref, projw_ref, trig_ref, mask_ref, kv_hbm,
    unperm_ref, wout_ref, resid_ref, wgu_hbm, wd_hbm,
    out_ref,
    tok_src, y_tok, tok_rows, send_qkv, y_qkv, keys_v, vals_v, q16, k16, v16, comb,
    send_att, y_att, att_rows, w_pad, send_proj, y_proj, ffn_src, y_ffn, ffn_rows, ffn_out,
    send_red, y_red, wgu_v, wd_v,
    tok_send, tok_recv, qkv_send, qkv_recv,
    att_send, att_recv, proj_send, proj_recv, ffn_send, ffn_recv, red_send, red_recv, w_sem,
):
    n_pages = kv_hbm.shape[0]
    keys_copy = pltpu.make_async_copy(kv_hbm.at[:, 0], keys_v.at[pl.ds(0, n_pages)], w_sem.at[0])
    vals_copy = pltpu.make_async_copy(kv_hbm.at[:, 1], vals_v.at[pl.ds(0, n_pages)], w_sem.at[1])
    wgu_copy = pltpu.make_async_copy(wgu_hbm, wgu_v, w_sem.at[2])
    wd_copy = pltpu.make_async_copy(wd_hbm, wd_v, w_sem.at[3])
    keys_copy.start()
    vals_copy.start()
    wgu_copy.start()
    wd_copy.start()

    wide = ("req", "kv")
    narrow = ("kv", "hid")
    wide_sizes, wide_me, wide_n = group_layout(wide)
    narrow_sizes, narrow_me, narrow_n = group_layout(narrow)
    half = narrow_n // 2
    barrier = pltpu.get_barrier_semaphore()
    for s in range(1, wide_n):
        peer = lax.rem(wide_me + s, wide_n)
        pl.semaphore_signal(
            barrier, inc=1, device_id=device_of(wide, wide_sizes, peer), device_id_type=MESH
        )
    for s in range(1, narrow_n):
        if s == half:
            continue
        peer = lax.rem(narrow_me + s, narrow_n)
        pl.semaphore_signal(
            barrier, inc=1, device_id=device_of(narrow, narrow_sizes, peer), device_id_type=MESH
        )

    n_req, per_pool, feature_width = tok_src.shape
    normed = rms_rows(tok_ref[...].astype(jnp.float32), gains_ref[0:1, :]).astype(jnp.bfloat16)
    for k in range(n_req):
        tok_src[k] = normed[:, feature_width * k : feature_width * (k + 1)]
    tok_rows[...] = jnp.zeros_like(tok_rows)
    pl.semaphore_wait(barrier, wide_n - 1 + narrow_n - 2)

    tok_me, tok_finish = start_copies(("req",), lambda k: tok_src.at[k], y_tok, tok_send, tok_recv)
    y_tok[tok_me] = tok_src[tok_me]
    tok_finish()
    for k in range(n_req):
        tok_rows[8 * k : 8 * k + per_pool, :] = y_tok[k].astype(jnp.float32)
    pooled = jnp.dot(
        order_ref[...], tok_rows[...].astype(jnp.bfloat16), preferred_element_type=jnp.float32
    ).astype(jnp.bfloat16)
    partial = jnp.dot(pooled, projw_ref[...], preferred_element_type=jnp.float32)
    for k in range(n_req):
        send_qkv[k] = partial[8 * k : 8 * k + per_pool]

    qkv_me, qkv_finish = start_copies(("req",), lambda k: send_qkv.at[k], y_qkv, qkv_send, qkv_recv)
    y_qkv[qkv_me] = send_qkv[qkv_me]
    qkv_finish()
    summed = y_qkv[0]
    for k in range(1, n_req):
        summed = summed + y_qkv[k]
    cosines = trig_ref[0]
    sines = trig_ref[1]
    head_width = q16.shape[1]
    half_width = head_width // 2

    def rot(v):
        a = v[:, :half_width]
        b = v[:, half_width:]
        return jnp.concatenate([a * cosines - b * sines, b * cosines + a * sines], axis=-1)

    per_group = q16.shape[0] // per_pool
    for h in range(per_group):
        qh = rot(rms_rows(summed[:, head_width * h : head_width * (h + 1)], qkg_ref[0:1, :]))
        q16[per_pool * h : per_pool * (h + 1), :] = qh.astype(jnp.bfloat16).astype(jnp.float32)
    split_at = per_group * head_width
    kn = rot(rms_rows(summed[:, split_at : split_at + head_width], qkg_ref[1:2, :]))
    kn = kn.astype(jnp.bfloat16).astype(jnp.float32)
    vn = rms_rows(summed[:, split_at + head_width :], 1.0)
    vn = vn.astype(jnp.bfloat16).astype(jnp.float32)
    for h in range(per_group):
        k16[per_pool * h : per_pool * (h + 1), :] = kn
        v16[per_pool * h : per_pool * (h + 1), :] = vn

    keys_copy.wait()
    vals_copy.wait()
    keys_v[n_pages] = jnp.zeros(keys_v.shape[1:], keys_v.dtype)
    vals_v[n_pages] = jnp.zeros(vals_v.shape[1:], vals_v.dtype)
    total_pos = keys_v.shape[0] * keys_v.shape[1]
    keys = keys_v[...].reshape(total_pos, head_width)
    vals = vals_v[...].reshape(total_pos, head_width)
    scale_factor = head_width ** (-0.5)
    q_f = q16[...]
    scores = lax.dot_general(
        q_f.astype(jnp.bfloat16), keys, (((1,), (1,)), ((), ())),
        preferred_element_type=jnp.float32,
    ) * scale_factor
    live = mask_ref[...] != 0
    masked = jnp.where(live, scores, neg_large)
    highest_cached = jnp.max(masked, axis=1, keepdims=True)
    weights = jnp.where(live, jnp.exp(masked - highest_cached), 0.0)
    totals = jnp.sum(weights, axis=1, keepdims=True)
    weighted = jnp.dot(weights.astype(jnp.bfloat16), vals, preferred_element_type=jnp.float32)
    own_score = jnp.sum(q_f * k16[...], axis=1, keepdims=True) * scale_factor
    highest = jnp.maximum(highest_cached, own_score)
    old_scale = jnp.exp(highest_cached - highest)
    new_scale = jnp.exp(own_score - highest)
    combined = (weighted * old_scale + new_scale * v16[...]) / (totals * old_scale + new_scale)
    comb[...] = combined.astype(jnp.bfloat16).astype(jnp.float32)
    slice_width = send_att.shape[2]
    per_head = head_width // slice_width
    for k in range(n_req):
        h, m = divmod(k, per_head)
        send_att[k] = comb[per_pool * h : per_pool * (h + 1), slice_width * m : slice_width * (m + 1)].astype(jnp.bfloat16)

    att_me, att_finish = start_copies(("req",), lambda k: send_att.at[k], y_att, att_send, att_recv)
    y_att[att_me] = send_att[att_me]
    att_rows[...] = jnp.zeros_like(att_rows)
    w_pad[...] = jnp.zeros_like(w_pad)
    rows_w = wout_ref.shape[0]
    w_pad[0:rows_w, :] = wout_ref[...]
    att_finish()
    for k in range(n_req):
        att_rows[8 * k : 8 * k + per_pool, 0:slice_width] = y_att[k].astype(jnp.float32)
    att_nat = jnp.dot(
        unperm_ref[...], att_rows[...].astype(jnp.bfloat16), preferred_element_type=jnp.float32
    ).astype(jnp.bfloat16)
    proj = jnp.dot(att_nat, w_pad[...], preferred_element_type=jnp.float32)
    n_wide, owned, width = send_proj.shape
    for q in range(n_wide):
        send_proj[q] = proj[owned * q : owned * (q + 1)].astype(jnp.bfloat16)

    proj_me, proj_finish = start_copies(wide, lambda k: send_proj.at[k], y_proj, proj_send, proj_recv)
    y_proj[proj_me] = send_proj[proj_me]
    proj_finish()
    projected = y_proj[0].astype(jnp.float32)
    for k in range(1, n_wide):
        projected = projected + y_proj[k].astype(jnp.float32)
    middle = (resid_ref[...] + rms_rows(projected, gains_ref[1:2, :])).astype(jnp.bfloat16)
    ffn_src[...] = rms_rows(middle.astype(jnp.float32), gains_ref[2:3, :]).astype(jnp.bfloat16)

    ffn_me, ffn_finish = start_copies(narrow, lambda k: ffn_src, y_ffn, ffn_send, ffn_recv)
    y_ffn[ffn_me] = ffn_src[...]
    ffn_finish()
    for k in range(narrow_n):
        ffn_rows[owned * k : owned * (k + 1), :] = y_ffn[k].astype(jnp.float32)
    wgu_copy.wait()
    wd_copy.wait()
    gate_up = jnp.dot(
        ffn_rows[...].astype(jnp.bfloat16), wgu_v[...], preferred_element_type=jnp.float32
    )
    hidden_width = wd_v.shape[0]
    hidden = (
        jax.nn.gelu(gate_up[:, :hidden_width], approximate=True) * gate_up[:, hidden_width:]
    ).astype(jnp.bfloat16)
    ffn_out[...] = jnp.dot(hidden, wd_v[...], preferred_element_type=jnp.float32)
    for k in range(narrow_n):
        send_red[k] = ffn_out[owned * k : owned * (k + 1), :].astype(jnp.bfloat16)

    red_me, red_finish = start_copies(narrow, lambda k: send_red.at[k], y_red, red_send, red_recv)
    y_red[red_me] = send_red[red_me]
    red_finish()
    ffn_sum = y_red[0].astype(jnp.float32)
    for k in range(1, narrow_n):
        ffn_sum = ffn_sum + y_red[k].astype(jnp.float32)
    out_ref[...] = (middle.astype(jnp.float32) + rms_rows(ffn_sum, gains_ref[3:4, :])).astype(
        out_ref.dtype
    )


def layer(tok, gains, qk_gains, order_pad, projw, trig, mask16, kv_cache,
          unperm, wout, residual, wgu, wd, cid):
    n_req = lax.axis_size("req")
    n_wide = n_req * lax.axis_size("kv")
    n_narrow = lax.axis_size("kv") * lax.axis_size("hid")
    owned, width = residual.shape
    per_pool = tok.shape[0]
    feature_width = width // n_req
    qkv_width = projw.shape[1]
    n_pages, _, page_size, head_width = kv_cache.shape
    slice_width = wout.shape[0]
    rows16 = mask16.shape[0]
    vmem = pl.BlockSpec(memory_space=pltpu.VMEM)
    anywhere = pl.BlockSpec(memory_space=pl.ANY)
    dma = pltpu.SemaphoreType.DMA
    f32 = jnp.float32
    bf16 = jnp.bfloat16
    return pl.pallas_call(
        layer_kernel,
        out_shape=jax.ShapeDtypeStruct((owned, width), bf16),
        in_specs=[vmem] * 7 + [anywhere] + [vmem] * 3 + [anywhere, anywhere],
        out_specs=vmem,
        scratch_shapes=[
            pltpu.VMEM((n_req, per_pool, feature_width), bf16),
            pltpu.VMEM((n_req, per_pool, feature_width), bf16),
            pltpu.VMEM((8 * n_req, feature_width), f32),
            pltpu.VMEM((n_req, per_pool, qkv_width), f32),
            pltpu.VMEM((n_req, per_pool, qkv_width), f32),
            pltpu.VMEM((n_pages + 1, page_size, head_width), bf16),
            pltpu.VMEM((n_pages + 1, page_size, head_width), bf16),
            pltpu.VMEM((rows16, head_width), f32),
            pltpu.VMEM((rows16, head_width), f32),
            pltpu.VMEM((rows16, head_width), f32),
            pltpu.VMEM((rows16, head_width), f32),
            pltpu.VMEM((n_req, per_pool, slice_width), bf16),
            pltpu.VMEM((n_req, per_pool, slice_width), bf16),
            pltpu.VMEM((8 * n_req, 128), f32),
            pltpu.VMEM((128, width), bf16),
            pltpu.VMEM((n_wide, owned, width), bf16),
            pltpu.VMEM((n_wide, owned, width), bf16),
            pltpu.VMEM((owned, width), bf16),
            pltpu.VMEM((n_narrow, owned, width), bf16),
            pltpu.VMEM((n_narrow * owned, width), f32),
            pltpu.VMEM((n_narrow * owned, width), f32),
            pltpu.VMEM((n_narrow, owned, width), bf16),
            pltpu.VMEM((n_narrow, owned, width), bf16),
            pltpu.VMEM(wgu.shape, bf16),
            pltpu.VMEM(wd.shape, bf16),
            dma((n_req,)), dma((n_req,)),
            dma((n_req,)), dma((n_req,)),
            dma((n_req,)), dma((n_req,)),
            dma((n_wide,)), dma((n_wide,)),
            dma((n_narrow,)), dma((n_narrow,)),
            dma((n_narrow,)), dma((n_narrow,)),
            dma((4,)),
        ],
        compiler_params=pltpu.CompilerParams(
            collective_id=cid, has_side_effects=True, vmem_limit_bytes=48 * 1024 * 1024
        ),
    )(tok, gains, qk_gains, order_pad, projw, trig, mask16, kv_cache,
      unperm, wout, residual, wgu, wd)

def rms_scale(value_entries, gain_row):
    mean_square = jnp.mean(value_entries * value_entries, axis=-1, keepdims=True)
    return value_entries * lax.rsqrt(mean_square + eps_norm) * gain_row


def rotate(value_entries, position):
    half_width = value_entries.shape[-1] // 2
    frequency = rope_base ** (
        -jnp.arange(half_width, dtype=jnp.float32) * 2.0 / value_entries.shape[-1]
    )
    angles = position[:, None, None] * frequency
    cosines = jnp.cos(angles)
    sines = jnp.sin(angles)
    first_half = value_entries[..., :half_width]
    second_half = value_entries[..., half_width:]
    return jnp.concatenate(
        [first_half * cosines - second_half * sines, second_half * cosines + first_half * sines],
        axis=-1,
    )


def shards(
    tokens,
    gains,
    qk_gains,
    w_query,
    key_value_weight,
    output_weight,
    w_gateup,
    w_down,
    kv_cache,
    lengths,
    page_table,
):
    req_position = lax.axis_index("req")
    kv_position = lax.axis_index("kv")
    hid_position = lax.axis_index("hid")
    req_total = lax.axis_size("req")
    hid_total = lax.axis_size("hid")
    kv_total = lax.axis_size("kv")
    rows_here, _, model_width = tokens.shape
    half_rows = rows_here // kv_total
    head_width = qk_gains.shape[1]
    per_group = w_query.shape[1] // head_width
    pool_size, _, page_size, _ = kv_cache.shape
    request_count = rows_here * req_total
    feature_width = w_query.shape[0]

    own_rows = tokens[:, 0, :]

    group_lengths = lax.dynamic_index_in_dim(lengths, hid_position, axis=1, keepdims=False)
    group_table = lax.dynamic_index_in_dim(page_table, hid_position, axis=1, keepdims=False)
    request_ids = jnp.arange(request_count, dtype=jnp.int32)
    pool_of = (group_table[:, 0] // pool_size) // hid_total
    pool_pos = pool_of * rows_here + request_ids % rows_here
    order = pool_pos[None, :] == request_ids[:, None]
    pad_to = 8 - rows_here
    order_pad = order.reshape(req_total, rows_here, req_total, rows_here)
    order_pad = jnp.pad(order_pad, ((0, 0), (0, pad_to), (0, 0), (0, pad_to)))
    order_pad = order_pad.reshape(8 * req_total, 8 * req_total).astype(jnp.bfloat16)
    unperm = order.T.reshape(request_count, req_total, rows_here)
    unperm = jnp.pad(unperm, ((0, 0), (0, 0), (0, pad_to)))
    unperm = unperm.reshape(request_count, 8 * req_total).astype(jnp.bfloat16)

    projection = jnp.concatenate(
        [w_query, key_value_weight.reshape(key_value_weight.shape[0], -1)], axis=1
    )

    mine = lax.dynamic_slice_in_dim(order, req_position * rows_here, rows_here, 0)
    my_lengths = jnp.sum(jnp.where(mine, group_lengths[None, :], 0), axis=1)
    my_tables = jnp.sum(jnp.where(mine[:, :, None], group_table[None, :, :], 0), axis=1)
    position = my_lengths.astype(jnp.float32)
    half_width = head_width // 2
    frequency = rope_base ** (-jnp.arange(half_width, dtype=jnp.float32) * 2.0 / head_width)
    angles = position[:, None] * frequency
    trig = jnp.stack([jnp.cos(angles), jnp.sin(angles)])

    slot_base = (req_position * hid_total + hid_position) * pool_size
    local = my_tables - slot_base
    slots = jnp.arange(pool_size, dtype=jnp.int32)
    match = local[:, :, None] == slots[None, None, :]
    page_ids = jnp.arange(my_tables.shape[1], dtype=jnp.int32)
    owner_hit = jnp.any(match, axis=1)
    page_of = jnp.sum(jnp.where(match, page_ids[None, :, None], 0), axis=(0, 1))
    cache_pos = page_of[:, None] * page_size + jnp.arange(page_size, dtype=jnp.int32)[None, :]
    live = owner_hit[:, :, None] & (cache_pos[None] < my_lengths[:, None, None])
    live = live.reshape(rows_here, pool_size * page_size)
    live = jnp.pad(live, ((0, 0), (0, page_size)))
    mask16 = jnp.tile(live, (per_group, 1)).astype(jnp.int32)

    residual = lax.dynamic_slice_in_dim(own_rows, kv_position * half_rows, half_rows, 0)
    hidden_width = w_down.shape[0]
    result = layer(
        own_rows,
        gains,
        qk_gains,
        order_pad,
        projection,
        trig,
        mask16,
        kv_cache,
        unperm,
        output_weight[0],
        residual.astype(jnp.float32),
        w_gateup.reshape(model_width, 2 * hidden_width),
        w_down,
        0,
    )
    return result[:, None, :]


def solution(mesh):
    return jax.shard_map(
        shards,
        mesh=mesh,
        in_specs=(
            P("req", "hid", None),
            P(),
            P(),
            P("req", "kv"),
            P("req", None, "kv"),
            P("kv", "req", None),
            P(None, None, ("kv", "hid")),
            P(("kv", "hid"), None),
            P(("req", "hid"), None, None, "kv"),
            P(),
            P(),
        ),
        out_specs=P(("req", "kv"), "hid", None),
        check_vma=False,
    )
```

```python
import functools

import jax
import jax.numpy as jnp
from jax import lax
from jax.experimental import pallas as pl
from jax.experimental.pallas import tpu as pltpu
from jax.sharding import PartitionSpec as P

eps_norm = 1e-06
rope_base = 1000000.0
neg_large = -1e30
MESH = pl.DeviceIdType.MESH
AXES = ("req", "kv", "hid")


def group_layout(group):
    sizes = [lax.axis_size(a) for a in group]
    me = 0
    for a, s in zip(group, sizes):
        me = me * s + lax.axis_index(a)
    total = 1
    for s in sizes:
        total *= s
    return sizes, me, total


def device_of(group, sizes, position):
    coords = {a: lax.axis_index(a) for a in AXES}
    rest = position
    for a, s in reversed(list(zip(group, sizes))):
        coords[a] = rest % s
        rest = rest // s
    return tuple(coords[a] for a in AXES)


def exchange_kernel(group, bcast, x_ref, y_ref, send_sem, recv_sem):
    sizes, me, n = group_layout(group)
    barrier = pltpu.get_barrier_semaphore()
    for s in range(1, n):
        peer = lax.rem(me + s, n)
        pl.semaphore_signal(
            barrier, inc=1, device_id=device_of(group, sizes, peer), device_id_type=MESH
        )
    pl.semaphore_wait(barrier, n - 1)
    copies = []
    for s in range(1, n):
        peer = lax.rem(me + s, n)
        src = x_ref if bcast else x_ref.at[peer]
        copy = pltpu.make_async_remote_copy(
            src_ref=src,
            dst_ref=y_ref.at[me],
            send_sem=send_sem.at[s],
            recv_sem=recv_sem.at[s],
            device_id=device_of(group, sizes, peer),
            device_id_type=MESH,
        )
        copy.start()
        copies.append(copy)
    if bcast:
        y_ref[me] = x_ref[...]
    else:
        y_ref[me] = x_ref[me]
    for s in range(1, n):
        copies[s - 1].wait_send()
        origin = lax.rem(me + n - s, n)
        src = x_ref if bcast else x_ref.at[origin]
        pltpu.make_async_remote_copy(
            src_ref=src,
            dst_ref=y_ref.at[origin],
            send_sem=send_sem.at[s],
            recv_sem=recv_sem.at[s],
            device_id=device_of(group, sizes, origin),
            device_id_type=MESH,
        ).wait_recv()


def exchange(x, group, cid, bcast=False):
    n = 1
    for a in group:
        n *= lax.axis_size(a)
    block = x.shape if bcast else x.shape[1:]
    return pl.pallas_call(
        functools.partial(exchange_kernel, group, bcast),
        out_shape=jax.ShapeDtypeStruct((n,) + tuple(block), x.dtype),
        in_specs=[pl.BlockSpec(memory_space=pltpu.VMEM)],
        out_specs=pl.BlockSpec(memory_space=pltpu.VMEM),
        scratch_shapes=[pltpu.SemaphoreType.DMA((n,)), pltpu.SemaphoreType.DMA((n,))],
        compiler_params=pltpu.CompilerParams(collective_id=cid, has_side_effects=True),
    )(x)


def start_copies(group, src_of, dst_ref, send_sem, recv_sem):
    sizes, me, n = group_layout(group)
    copies = []
    for s in range(1, n):
        peer = lax.rem(me + s, n)
        copy = pltpu.make_async_remote_copy(
            src_ref=src_of(peer),
            dst_ref=dst_ref.at[me],
            send_sem=send_sem.at[s],
            recv_sem=recv_sem.at[s],
            device_id=device_of(group, sizes, peer),
            device_id_type=MESH,
        )
        copy.start()
        copies.append(copy)

    def finish():
        for s in range(1, n):
            copies[s - 1].wait_send()
            origin = lax.rem(me + n - s, n)
            pltpu.make_async_remote_copy(
                src_ref=src_of(origin),
                dst_ref=dst_ref.at[origin],
                send_sem=send_sem.at[s],
                recv_sem=recv_sem.at[s],
                device_id=device_of(group, sizes, origin),
                device_id_type=MESH,
            ).wait_recv()

    return me, finish


def rms_rows(value_entries, gain_row):
    mean_square = jnp.mean(value_entries * value_entries, axis=-1, keepdims=True)
    return value_entries * lax.rsqrt(mean_square + eps_norm) * gain_row


def layer_kernel(
    tok_ref, gains_ref, qkg_ref, order_ref, projw_ref, trig_ref, mask_ref, kv_hbm,
    unperm_ref, wout_ref, resid_ref, wgu_ref, wd_hbm,
    out_ref,
    tok_src, y_tok, tok_rows, send_qkv, y_qkv, keys_v, vals_v, q16, k16, v16, comb,
    send_att, y_att, att_rows, w_pad, send_proj, y_proj, ffn_src, y_ffn, ffn_rows, ffn_out,
    send_red, y_red, wgu_v, wd_v,
    tok_send, tok_recv, qkv_send, qkv_recv,
    att_send, att_recv, proj_send, proj_recv, ffn_send, ffn_recv, red_send, red_recv, w_sem,
):
    n_pages = kv_hbm.shape[0]
    keys_copy = pltpu.make_async_copy(kv_hbm.at[:, 0], keys_v.at[pl.ds(0, n_pages)], w_sem.at[0])
    vals_copy = pltpu.make_async_copy(kv_hbm.at[:, 1], vals_v.at[pl.ds(0, n_pages)], w_sem.at[1])
    wd_copy = pltpu.make_async_copy(wd_hbm, wd_v, w_sem.at[3])
    keys_copy.start()
    vals_copy.start()
    wd_copy.start()

    wide = ("req", "kv")
    narrow = ("kv", "hid")
    wide_sizes, wide_me, wide_n = group_layout(wide)
    narrow_sizes, narrow_me, narrow_n = group_layout(narrow)
    half = narrow_n // 2
    barrier = pltpu.get_barrier_semaphore()
    for s in range(1, wide_n):
        peer = lax.rem(wide_me + s, wide_n)
        pl.semaphore_signal(
            barrier, inc=1, device_id=device_of(wide, wide_sizes, peer), device_id_type=MESH
        )
    for s in range(1, narrow_n):
        if s == half:
            continue
        peer = lax.rem(narrow_me + s, narrow_n)
        pl.semaphore_signal(
            barrier, inc=1, device_id=device_of(narrow, narrow_sizes, peer), device_id_type=MESH
        )

    n_req, per_pool, feature_width = tok_src.shape
    normed = rms_rows(tok_ref[...].astype(jnp.float32), gains_ref[0:1, :]).astype(jnp.bfloat16)
    for k in range(n_req):
        tok_src[k] = normed[:, feature_width * k : feature_width * (k + 1)]
    tok_rows[...] = jnp.zeros_like(tok_rows)
    pl.semaphore_wait(barrier, wide_n - 1 + narrow_n - 2)

    tok_me, tok_finish = start_copies(("req",), lambda k: tok_src.at[k], y_tok, tok_send, tok_recv)
    y_tok[tok_me] = tok_src[tok_me]
    tok_finish()
    for k in range(n_req):
        tok_rows[8 * k : 8 * k + per_pool, :] = y_tok[k].astype(jnp.float32)
    pooled = jnp.dot(
        order_ref[...], tok_rows[...].astype(jnp.bfloat16), preferred_element_type=jnp.float32
    ).astype(jnp.bfloat16)
    partial = jnp.dot(pooled, projw_ref[...], preferred_element_type=jnp.float32)
    for k in range(n_req):
        send_qkv[k] = partial[8 * k : 8 * k + per_pool]

    qkv_me, qkv_finish = start_copies(("req",), lambda k: send_qkv.at[k], y_qkv, qkv_send, qkv_recv)
    y_qkv[qkv_me] = send_qkv[qkv_me]
    qkv_finish()
    summed = y_qkv[0]
    for k in range(1, n_req):
        summed = summed + y_qkv[k]
    cosines = trig_ref[0]
    sines = trig_ref[1]
    head_width = q16.shape[1]
    half_width = head_width // 2

    def rot(v):
        a = v[:, :half_width]
        b = v[:, half_width:]
        return jnp.concatenate([a * cosines - b * sines, b * cosines + a * sines], axis=-1)

    per_group = q16.shape[0] // per_pool
    for h in range(per_group):
        qh = rot(rms_rows(summed[:, head_width * h : head_width * (h + 1)], qkg_ref[0:1, :]))
        q16[per_pool * h : per_pool * (h + 1), :] = qh.astype(jnp.bfloat16).astype(jnp.float32)
    split_at = per_group * head_width
    kn = rot(rms_rows(summed[:, split_at : split_at + head_width], qkg_ref[1:2, :]))
    kn = kn.astype(jnp.bfloat16).astype(jnp.float32)
    vn = rms_rows(summed[:, split_at + head_width :], 1.0)
    vn = vn.astype(jnp.bfloat16).astype(jnp.float32)
    for h in range(per_group):
        k16[per_pool * h : per_pool * (h + 1), :] = kn
        v16[per_pool * h : per_pool * (h + 1), :] = vn

    keys_copy.wait()
    vals_copy.wait()
    keys_v[n_pages] = jnp.zeros(keys_v.shape[1:], keys_v.dtype)
    vals_v[n_pages] = jnp.zeros(vals_v.shape[1:], vals_v.dtype)
    total_pos = keys_v.shape[0] * keys_v.shape[1]
    keys = keys_v[...].reshape(total_pos, head_width)
    vals = vals_v[...].reshape(total_pos, head_width)
    scale_factor = head_width ** (-0.5)
    q_f = q16[...]
    scores = lax.dot_general(
        q_f.astype(jnp.bfloat16), keys, (((1,), (1,)), ((), ())),
        preferred_element_type=jnp.float32,
    ) * scale_factor
    live = mask_ref[...] != 0
    masked = jnp.where(live, scores, neg_large)
    highest_cached = jnp.max(masked, axis=1, keepdims=True)
    weights = jnp.where(live, jnp.exp(masked - highest_cached), 0.0)
    totals = jnp.sum(weights, axis=1, keepdims=True)
    weighted = jnp.dot(weights.astype(jnp.bfloat16), vals, preferred_element_type=jnp.float32)
    own_score = jnp.sum(q_f * k16[...], axis=1, keepdims=True) * scale_factor
    highest = jnp.maximum(highest_cached, own_score)
    old_scale = jnp.exp(highest_cached - highest)
    new_scale = jnp.exp(own_score - highest)
    combined = (weighted * old_scale + new_scale * v16[...]) / (totals * old_scale + new_scale)
    comb[...] = combined.astype(jnp.bfloat16).astype(jnp.float32)
    slice_width = send_att.shape[2]
    per_head = head_width // slice_width
    for k in range(n_req):
        h, m = divmod(k, per_head)
        send_att[k] = comb[per_pool * h : per_pool * (h + 1), slice_width * m : slice_width * (m + 1)].astype(jnp.bfloat16)

    att_me, att_finish = start_copies(("req",), lambda k: send_att.at[k], y_att, att_send, att_recv)
    y_att[att_me] = send_att[att_me]
    att_rows[...] = jnp.zeros_like(att_rows)
    w_pad[...] = jnp.zeros_like(w_pad)
    rows_w = wout_ref.shape[0]
    w_pad[0:rows_w, :] = wout_ref[...]
    att_finish()
    for k in range(n_req):
        att_rows[8 * k : 8 * k + per_pool, 0:slice_width] = y_att[k].astype(jnp.float32)
    att_nat = jnp.dot(
        unperm_ref[...], att_rows[...].astype(jnp.bfloat16), preferred_element_type=jnp.float32
    ).astype(jnp.bfloat16)
    proj = jnp.dot(att_nat, w_pad[...], preferred_element_type=jnp.float32)
    n_wide, owned, width = send_proj.shape
    for q in range(n_wide):
        send_proj[q] = proj[owned * q : owned * (q + 1)].astype(jnp.bfloat16)

    proj_me, proj_finish = start_copies(wide, lambda k: send_proj.at[k], y_proj, proj_send, proj_recv)
    y_proj[proj_me] = send_proj[proj_me]
    proj_finish()
    projected = y_proj[0].astype(jnp.float32)
    for k in range(1, n_wide):
        projected = projected + y_proj[k].astype(jnp.float32)
    middle = (resid_ref[...] + rms_rows(projected, gains_ref[1:2, :])).astype(jnp.bfloat16)
    ffn_src[...] = rms_rows(middle.astype(jnp.float32), gains_ref[2:3, :]).astype(jnp.bfloat16)

    ffn_me, ffn_finish = start_copies(narrow, lambda k: ffn_src, y_ffn, ffn_send, ffn_recv)
    y_ffn[ffn_me] = ffn_src[...]
    ffn_finish()
    for k in range(narrow_n):
        ffn_rows[owned * k : owned * (k + 1), :] = y_ffn[k].astype(jnp.float32)
    wd_copy.wait()
    ffn_x = ffn_rows[...].astype(jnp.bfloat16)
    gate = jnp.dot(ffn_x, wgu_ref[:, 0, :], preferred_element_type=jnp.float32)
    up = jnp.dot(ffn_x, wgu_ref[:, 1, :], preferred_element_type=jnp.float32)
    hidden = (jax.nn.gelu(gate, approximate=True) * up).astype(jnp.bfloat16)
    ffn_out[...] = jnp.dot(hidden, wd_v[...], preferred_element_type=jnp.float32)
    for k in range(narrow_n):
        send_red[k] = ffn_out[owned * k : owned * (k + 1), :].astype(jnp.bfloat16)

    red_me, red_finish = start_copies(narrow, lambda k: send_red.at[k], y_red, red_send, red_recv)
    y_red[red_me] = send_red[red_me]
    red_finish()
    ffn_sum = y_red[0].astype(jnp.float32)
    for k in range(1, narrow_n):
        ffn_sum = ffn_sum + y_red[k].astype(jnp.float32)
    out_ref[...] = (middle.astype(jnp.float32) + rms_rows(ffn_sum, gains_ref[3:4, :])).astype(
        out_ref.dtype
    )


def layer(tok, gains, qk_gains, order_pad, projw, trig, mask16, kv_cache,
          unperm, wout, residual, wgu, wd, cid):
    n_req = lax.axis_size("req")
    n_wide = n_req * lax.axis_size("kv")
    n_narrow = lax.axis_size("kv") * lax.axis_size("hid")
    owned, width = residual.shape
    per_pool = tok.shape[0]
    feature_width = width // n_req
    qkv_width = projw.shape[1]
    n_pages, _, page_size, head_width = kv_cache.shape
    slice_width = wout.shape[0]
    rows16 = mask16.shape[0]
    vmem = pl.BlockSpec(memory_space=pltpu.VMEM)
    anywhere = pl.BlockSpec(memory_space=pl.ANY)
    dma = pltpu.SemaphoreType.DMA
    f32 = jnp.float32
    bf16 = jnp.bfloat16
    return pl.pallas_call(
        layer_kernel,
        out_shape=jax.ShapeDtypeStruct((owned, width), bf16),
        in_specs=[vmem] * 7 + [anywhere] + [vmem] * 4 + [anywhere],
        out_specs=vmem,
        scratch_shapes=[
            pltpu.VMEM((n_req, per_pool, feature_width), bf16),
            pltpu.VMEM((n_req, per_pool, feature_width), bf16),
            pltpu.VMEM((8 * n_req, feature_width), f32),
            pltpu.VMEM((n_req, per_pool, qkv_width), f32),
            pltpu.VMEM((n_req, per_pool, qkv_width), f32),
            pltpu.VMEM((n_pages + 1, page_size, head_width), bf16),
            pltpu.VMEM((n_pages + 1, page_size, head_width), bf16),
            pltpu.VMEM((rows16, head_width), f32),
            pltpu.VMEM((rows16, head_width), f32),
            pltpu.VMEM((rows16, head_width), f32),
            pltpu.VMEM((rows16, head_width), f32),
            pltpu.VMEM((n_req, per_pool, slice_width), bf16),
            pltpu.VMEM((n_req, per_pool, slice_width), bf16),
            pltpu.VMEM((8 * n_req, 128), f32),
            pltpu.VMEM((128, width), bf16),
            pltpu.VMEM((n_wide, owned, width), bf16),
            pltpu.VMEM((n_wide, owned, width), bf16),
            pltpu.VMEM((owned, width), bf16),
            pltpu.VMEM((n_narrow, owned, width), bf16),
            pltpu.VMEM((n_narrow * owned, width), f32),
            pltpu.VMEM((n_narrow * owned, width), f32),
            pltpu.VMEM((n_narrow, owned, width), bf16),
            pltpu.VMEM((n_narrow, owned, width), bf16),
            pltpu.VMEM((8, 128), bf16),
            pltpu.VMEM(wd.shape, bf16),
            dma((n_req,)), dma((n_req,)),
            dma((n_req,)), dma((n_req,)),
            dma((n_req,)), dma((n_req,)),
            dma((n_wide,)), dma((n_wide,)),
            dma((n_narrow,)), dma((n_narrow,)),
            dma((n_narrow,)), dma((n_narrow,)),
            dma((4,)),
        ],
        compiler_params=pltpu.CompilerParams(
            collective_id=cid, has_side_effects=True, vmem_limit_bytes=48 * 1024 * 1024
        ),
    )(tok, gains, qk_gains, order_pad, projw, trig, mask16, kv_cache,
      unperm, wout, residual, wgu, wd)

def rms_scale(value_entries, gain_row):
    mean_square = jnp.mean(value_entries * value_entries, axis=-1, keepdims=True)
    return value_entries * lax.rsqrt(mean_square + eps_norm) * gain_row


def rotate(value_entries, position):
    half_width = value_entries.shape[-1] // 2
    frequency = rope_base ** (
        -jnp.arange(half_width, dtype=jnp.float32) * 2.0 / value_entries.shape[-1]
    )
    angles = position[:, None, None] * frequency
    cosines = jnp.cos(angles)
    sines = jnp.sin(angles)
    first_half = value_entries[..., :half_width]
    second_half = value_entries[..., half_width:]
    return jnp.concatenate(
        [first_half * cosines - second_half * sines, second_half * cosines + first_half * sines],
        axis=-1,
    )


def shards(
    tokens,
    gains,
    qk_gains,
    w_query,
    key_value_weight,
    output_weight,
    w_gateup,
    w_down,
    kv_cache,
    lengths,
    page_table,
):
    req_position = lax.axis_index("req")
    kv_position = lax.axis_index("kv")
    hid_position = lax.axis_index("hid")
    req_total = lax.axis_size("req")
    hid_total = lax.axis_size("hid")
    kv_total = lax.axis_size("kv")
    rows_here, _, model_width = tokens.shape
    half_rows = rows_here // kv_total
    head_width = qk_gains.shape[1]
    per_group = w_query.shape[1] // head_width
    pool_size, _, page_size, _ = kv_cache.shape
    request_count = rows_here * req_total
    feature_width = w_query.shape[0]

    own_rows = tokens[:, 0, :]

    group_lengths = lax.dynamic_index_in_dim(lengths, hid_position, axis=1, keepdims=False)
    group_table = lax.dynamic_index_in_dim(page_table, hid_position, axis=1, keepdims=False)
    request_ids = jnp.arange(request_count, dtype=jnp.int32)
    pool_of = (group_table[:, 0] // pool_size) // hid_total
    pool_pos = pool_of * rows_here + request_ids % rows_here
    order = pool_pos[None, :] == request_ids[:, None]
    pad_to = 8 - rows_here
    order_pad = order.reshape(req_total, rows_here, req_total, rows_here)
    order_pad = jnp.pad(order_pad, ((0, 0), (0, pad_to), (0, 0), (0, pad_to)))
    order_pad = order_pad.reshape(8 * req_total, 8 * req_total).astype(jnp.bfloat16)
    unperm = order.T.reshape(request_count, req_total, rows_here)
    unperm = jnp.pad(unperm, ((0, 0), (0, 0), (0, pad_to)))
    unperm = unperm.reshape(request_count, 8 * req_total).astype(jnp.bfloat16)

    projection = jnp.concatenate(
        [w_query, key_value_weight.reshape(key_value_weight.shape[0], -1)], axis=1
    )

    mine = lax.dynamic_slice_in_dim(order, req_position * rows_here, rows_here, 0)
    my_lengths = jnp.sum(jnp.where(mine, group_lengths[None, :], 0), axis=1)
    my_tables = jnp.sum(jnp.where(mine[:, :, None], group_table[None, :, :], 0), axis=1)
    position = my_lengths.astype(jnp.float32)
    half_width = head_width // 2
    frequency = rope_base ** (-jnp.arange(half_width, dtype=jnp.float32) * 2.0 / head_width)
    angles = position[:, None] * frequency
    trig = jnp.stack([jnp.cos(angles), jnp.sin(angles)])

    slot_base = (req_position * hid_total + hid_position) * pool_size
    local = my_tables - slot_base
    slots = jnp.arange(pool_size, dtype=jnp.int32)
    match = local[:, :, None] == slots[None, None, :]
    page_ids = jnp.arange(my_tables.shape[1], dtype=jnp.int32)
    owner_hit = jnp.any(match, axis=1)
    page_of = jnp.sum(jnp.where(match, page_ids[None, :, None], 0), axis=(0, 1))
    cache_pos = page_of[:, None] * page_size + jnp.arange(page_size, dtype=jnp.int32)[None, :]
    live = owner_hit[:, :, None] & (cache_pos[None] < my_lengths[:, None, None])
    live = live.reshape(rows_here, pool_size * page_size)
    live = jnp.pad(live, ((0, 0), (0, page_size)))
    mask16 = jnp.tile(live, (per_group, 1)).astype(jnp.int32)

    residual = lax.dynamic_slice_in_dim(own_rows, kv_position * half_rows, half_rows, 0)
    hidden_width = w_down.shape[0]
    result = layer(
        own_rows,
        gains,
        qk_gains,
        order_pad,
        projection,
        trig,
        mask16,
        kv_cache,
        unperm,
        output_weight[0],
        residual.astype(jnp.float32),
        w_gateup,
        w_down,
        0,
    )
    return result[:, None, :]


def solution(mesh):
    return jax.shard_map(
        shards,
        mesh=mesh,
        in_specs=(
            P("req", "hid", None),
            P(),
            P(),
            P("req", "kv"),
            P("req", None, "kv"),
            P("kv", "req", None),
            P(None, None, ("kv", "hid")),
            P(("kv", "hid"), None),
            P(("req", "hid"), None, None, "kv"),
            P(),
            P(),
        ),
        out_specs=P(("req", "kv"), "hid", None),
        check_vma=False,
    )
```

```python
import functools

import jax
import jax.numpy as jnp
from jax import lax
from jax.experimental import pallas as pl
from jax.experimental.pallas import tpu as pltpu
from jax.sharding import PartitionSpec as P

eps_norm = 1e-06
rope_base = 1000000.0
neg_large = -1e30
MESH = pl.DeviceIdType.MESH
AXES = ("req", "kv", "hid")


def group_layout(group):
    sizes = [lax.axis_size(a) for a in group]
    me = 0
    for a, s in zip(group, sizes):
        me = me * s + lax.axis_index(a)
    total = 1
    for s in sizes:
        total *= s
    return sizes, me, total


def device_of(group, sizes, position):
    coords = {a: lax.axis_index(a) for a in AXES}
    rest = position
    for a, s in reversed(list(zip(group, sizes))):
        coords[a] = rest % s
        rest = rest // s
    return tuple(coords[a] for a in AXES)


def exchange_kernel(group, bcast, x_ref, y_ref, send_sem, recv_sem):
    sizes, me, n = group_layout(group)
    barrier = pltpu.get_barrier_semaphore()
    for s in range(1, n):
        peer = lax.rem(me + s, n)
        pl.semaphore_signal(
            barrier, inc=1, device_id=device_of(group, sizes, peer), device_id_type=MESH
        )
    pl.semaphore_wait(barrier, n - 1)
    copies = []
    for s in range(1, n):
        peer = lax.rem(me + s, n)
        src = x_ref if bcast else x_ref.at[peer]
        copy = pltpu.make_async_remote_copy(
            src_ref=src,
            dst_ref=y_ref.at[me],
            send_sem=send_sem.at[s],
            recv_sem=recv_sem.at[s],
            device_id=device_of(group, sizes, peer),
            device_id_type=MESH,
        )
        copy.start()
        copies.append(copy)
    if bcast:
        y_ref[me] = x_ref[...]
    else:
        y_ref[me] = x_ref[me]
    for s in range(1, n):
        copies[s - 1].wait_send()
        origin = lax.rem(me + n - s, n)
        src = x_ref if bcast else x_ref.at[origin]
        pltpu.make_async_remote_copy(
            src_ref=src,
            dst_ref=y_ref.at[origin],
            send_sem=send_sem.at[s],
            recv_sem=recv_sem.at[s],
            device_id=device_of(group, sizes, origin),
            device_id_type=MESH,
        ).wait_recv()


def exchange(x, group, cid, bcast=False):
    n = 1
    for a in group:
        n *= lax.axis_size(a)
    block = x.shape if bcast else x.shape[1:]
    return pl.pallas_call(
        functools.partial(exchange_kernel, group, bcast),
        out_shape=jax.ShapeDtypeStruct((n,) + tuple(block), x.dtype),
        in_specs=[pl.BlockSpec(memory_space=pltpu.VMEM)],
        out_specs=pl.BlockSpec(memory_space=pltpu.VMEM),
        scratch_shapes=[pltpu.SemaphoreType.DMA((n,)), pltpu.SemaphoreType.DMA((n,))],
        compiler_params=pltpu.CompilerParams(collective_id=cid, has_side_effects=True),
    )(x)


def start_copies(group, src_of, dst_ref, send_sem, recv_sem):
    sizes, me, n = group_layout(group)
    copies = []
    for s in range(1, n):
        peer = lax.rem(me + s, n)
        copy = pltpu.make_async_remote_copy(
            src_ref=src_of(peer),
            dst_ref=dst_ref.at[me],
            send_sem=send_sem.at[s],
            recv_sem=recv_sem.at[s],
            device_id=device_of(group, sizes, peer),
            device_id_type=MESH,
        )
        copy.start()
        copies.append(copy)

    def finish():
        for s in range(1, n):
            copies[s - 1].wait_send()
            origin = lax.rem(me + n - s, n)
            pltpu.make_async_remote_copy(
                src_ref=src_of(origin),
                dst_ref=dst_ref.at[origin],
                send_sem=send_sem.at[s],
                recv_sem=recv_sem.at[s],
                device_id=device_of(group, sizes, origin),
                device_id_type=MESH,
            ).wait_recv()

    return me, finish


def rms_rows(value_entries, gain_row):
    mean_square = jnp.mean(value_entries * value_entries, axis=-1, keepdims=True)
    return value_entries * lax.rsqrt(mean_square + eps_norm) * gain_row


def unpack_rows(wgu_raw, wgu_v, start, count):
    hidden_width = wgu_raw.shape[2]
    rows = pl.ds(start, count)
    wgu_v[rows, 0:hidden_width] = wgu_raw[rows, 0, :]
    wgu_v[rows, hidden_width:] = wgu_raw[rows, 1, :]


def layer_kernel(
    tok_ref, gains_ref, qkg_ref, order_ref, projw_ref, trig_ref, mask_ref, kv_hbm,
    unperm_ref, wout_ref, resid_ref, wgu_hbm, wd_hbm,
    out_ref,
    tok_src, y_tok, tok_rows, send_qkv, y_qkv, keys_v, vals_v, q16, k16, v16, comb,
    send_att, y_att, att_rows, w_pad, send_proj, y_proj, ffn_src, y_ffn, ffn_rows, ffn_out,
    send_red, y_red, wgu_v, wd_v, wgu_raw,
    tok_send, tok_recv, qkv_send, qkv_recv,
    att_send, att_recv, proj_send, proj_recv, ffn_send, ffn_recv, red_send, red_recv, w_sem,
):
    n_pages = kv_hbm.shape[0]
    keys_copy = pltpu.make_async_copy(kv_hbm.at[:, 0], keys_v.at[pl.ds(0, n_pages)], w_sem.at[0])
    vals_copy = pltpu.make_async_copy(kv_hbm.at[:, 1], vals_v.at[pl.ds(0, n_pages)], w_sem.at[1])
    wgu_copy = pltpu.make_async_copy(wgu_hbm, wgu_raw, w_sem.at[2])
    wd_copy = pltpu.make_async_copy(wd_hbm, wd_v, w_sem.at[3])
    keys_copy.start()
    vals_copy.start()
    wgu_copy.start()
    wd_copy.start()

    wide = ("req", "kv")
    narrow = ("kv", "hid")
    wide_sizes, wide_me, wide_n = group_layout(wide)
    narrow_sizes, narrow_me, narrow_n = group_layout(narrow)
    half = narrow_n // 2
    barrier = pltpu.get_barrier_semaphore()
    for s in range(1, wide_n):
        peer = lax.rem(wide_me + s, wide_n)
        pl.semaphore_signal(
            barrier, inc=1, device_id=device_of(wide, wide_sizes, peer), device_id_type=MESH
        )
    for s in range(1, narrow_n):
        if s == half:
            continue
        peer = lax.rem(narrow_me + s, narrow_n)
        pl.semaphore_signal(
            barrier, inc=1, device_id=device_of(narrow, narrow_sizes, peer), device_id_type=MESH
        )

    n_req, per_pool, feature_width = tok_src.shape
    normed = rms_rows(tok_ref[...].astype(jnp.float32), gains_ref[0:1, :]).astype(jnp.bfloat16)
    for k in range(n_req):
        tok_src[k] = normed[:, feature_width * k : feature_width * (k + 1)]
    tok_rows[...] = jnp.zeros_like(tok_rows)
    pl.semaphore_wait(barrier, wide_n - 1 + narrow_n - 2)

    tok_me, tok_finish = start_copies(("req",), lambda k: tok_src.at[k], y_tok, tok_send, tok_recv)
    y_tok[tok_me] = tok_src[tok_me]
    wgu_copy.wait()
    unpack_rows(wgu_raw, wgu_v, 0, 512)
    tok_finish()
    for k in range(n_req):
        tok_rows[8 * k : 8 * k + per_pool, :] = y_tok[k].astype(jnp.float32)
    pooled = jnp.dot(
        order_ref[...], tok_rows[...].astype(jnp.bfloat16), preferred_element_type=jnp.float32
    ).astype(jnp.bfloat16)
    partial = jnp.dot(pooled, projw_ref[...], preferred_element_type=jnp.float32)
    for k in range(n_req):
        send_qkv[k] = partial[8 * k : 8 * k + per_pool]

    qkv_me, qkv_finish = start_copies(("req",), lambda k: send_qkv.at[k], y_qkv, qkv_send, qkv_recv)
    y_qkv[qkv_me] = send_qkv[qkv_me]
    unpack_rows(wgu_raw, wgu_v, 512, 512)
    qkv_finish()
    summed = y_qkv[0]
    for k in range(1, n_req):
        summed = summed + y_qkv[k]
    cosines = trig_ref[0]
    sines = trig_ref[1]
    head_width = q16.shape[1]
    half_width = head_width // 2

    def rot(v):
        a = v[:, :half_width]
        b = v[:, half_width:]
        return jnp.concatenate([a * cosines - b * sines, b * cosines + a * sines], axis=-1)

    per_group = q16.shape[0] // per_pool
    for h in range(per_group):
        qh = rot(rms_rows(summed[:, head_width * h : head_width * (h + 1)], qkg_ref[0:1, :]))
        q16[per_pool * h : per_pool * (h + 1), :] = qh.astype(jnp.bfloat16).astype(jnp.float32)
    split_at = per_group * head_width
    kn = rot(rms_rows(summed[:, split_at : split_at + head_width], qkg_ref[1:2, :]))
    kn = kn.astype(jnp.bfloat16).astype(jnp.float32)
    vn = rms_rows(summed[:, split_at + head_width :], 1.0)
    vn = vn.astype(jnp.bfloat16).astype(jnp.float32)
    for h in range(per_group):
        k16[per_pool * h : per_pool * (h + 1), :] = kn
        v16[per_pool * h : per_pool * (h + 1), :] = vn

    keys_copy.wait()
    vals_copy.wait()
    keys_v[n_pages] = jnp.zeros(keys_v.shape[1:], keys_v.dtype)
    vals_v[n_pages] = jnp.zeros(vals_v.shape[1:], vals_v.dtype)
    total_pos = keys_v.shape[0] * keys_v.shape[1]
    keys = keys_v[...].reshape(total_pos, head_width)
    vals = vals_v[...].reshape(total_pos, head_width)
    scale_factor = head_width ** (-0.5)
    q_f = q16[...]
    scores = lax.dot_general(
        q_f.astype(jnp.bfloat16), keys, (((1,), (1,)), ((), ())),
        preferred_element_type=jnp.float32,
    ) * scale_factor
    live = mask_ref[...] != 0
    masked = jnp.where(live, scores, neg_large)
    highest_cached = jnp.max(masked, axis=1, keepdims=True)
    weights = jnp.where(live, jnp.exp(masked - highest_cached), 0.0)
    totals = jnp.sum(weights, axis=1, keepdims=True)
    weighted = jnp.dot(weights.astype(jnp.bfloat16), vals, preferred_element_type=jnp.float32)
    own_score = jnp.sum(q_f * k16[...], axis=1, keepdims=True) * scale_factor
    highest = jnp.maximum(highest_cached, own_score)
    old_scale = jnp.exp(highest_cached - highest)
    new_scale = jnp.exp(own_score - highest)
    combined = (weighted * old_scale + new_scale * v16[...]) / (totals * old_scale + new_scale)
    comb[...] = combined.astype(jnp.bfloat16).astype(jnp.float32)
    slice_width = send_att.shape[2]
    per_head = head_width // slice_width
    for k in range(n_req):
        h, m = divmod(k, per_head)
        send_att[k] = comb[per_pool * h : per_pool * (h + 1), slice_width * m : slice_width * (m + 1)].astype(jnp.bfloat16)

    att_me, att_finish = start_copies(("req",), lambda k: send_att.at[k], y_att, att_send, att_recv)
    y_att[att_me] = send_att[att_me]
    att_rows[...] = jnp.zeros_like(att_rows)
    w_pad[...] = jnp.zeros_like(w_pad)
    rows_w = wout_ref.shape[0]
    w_pad[0:rows_w, :] = wout_ref[...]
    unpack_rows(wgu_raw, wgu_v, 1024, 512)
    att_finish()
    for k in range(n_req):
        att_rows[8 * k : 8 * k + per_pool, 0:slice_width] = y_att[k].astype(jnp.float32)
    att_nat = jnp.dot(
        unperm_ref[...], att_rows[...].astype(jnp.bfloat16), preferred_element_type=jnp.float32
    ).astype(jnp.bfloat16)
    proj = jnp.dot(att_nat, w_pad[...], preferred_element_type=jnp.float32)
    n_wide, owned, width = send_proj.shape
    for q in range(n_wide):
        send_proj[q] = proj[owned * q : owned * (q + 1)].astype(jnp.bfloat16)

    proj_me, proj_finish = start_copies(wide, lambda k: send_proj.at[k], y_proj, proj_send, proj_recv)
    y_proj[proj_me] = send_proj[proj_me]
    unpack_rows(wgu_raw, wgu_v, 1536, 512)
    proj_finish()
    projected = y_proj[0].astype(jnp.float32)
    for k in range(1, n_wide):
        projected = projected + y_proj[k].astype(jnp.float32)
    middle = (resid_ref[...] + rms_rows(projected, gains_ref[1:2, :])).astype(jnp.bfloat16)
    ffn_src[...] = rms_rows(middle.astype(jnp.float32), gains_ref[2:3, :]).astype(jnp.bfloat16)

    ffn_me, ffn_finish = start_copies(narrow, lambda k: ffn_src, y_ffn, ffn_send, ffn_recv)
    y_ffn[ffn_me] = ffn_src[...]
    ffn_finish()
    for k in range(narrow_n):
        ffn_rows[owned * k : owned * (k + 1), :] = y_ffn[k].astype(jnp.float32)
    wd_copy.wait()
    gate_up = jnp.dot(
        ffn_rows[...].astype(jnp.bfloat16), wgu_v[...], preferred_element_type=jnp.float32
    )
    hidden_width = wd_v.shape[0]
    hidden = (
        jax.nn.gelu(gate_up[:, :hidden_width], approximate=True) * gate_up[:, hidden_width:]
    ).astype(jnp.bfloat16)
    ffn_out[...] = jnp.dot(hidden, wd_v[...], preferred_element_type=jnp.float32)
    for k in range(narrow_n):
        send_red[k] = ffn_out[owned * k : owned * (k + 1), :].astype(jnp.bfloat16)

    red_me, red_finish = start_copies(narrow, lambda k: send_red.at[k], y_red, red_send, red_recv)
    y_red[red_me] = send_red[red_me]
    red_finish()
    ffn_sum = y_red[0].astype(jnp.float32)
    for k in range(1, narrow_n):
        ffn_sum = ffn_sum + y_red[k].astype(jnp.float32)
    out_ref[...] = (middle.astype(jnp.float32) + rms_rows(ffn_sum, gains_ref[3:4, :])).astype(
        out_ref.dtype
    )


def layer(tok, gains, qk_gains, order_pad, projw, trig, mask16, kv_cache,
          unperm, wout, residual, wgu, wd, cid):
    n_req = lax.axis_size("req")
    n_wide = n_req * lax.axis_size("kv")
    n_narrow = lax.axis_size("kv") * lax.axis_size("hid")
    owned, width = residual.shape
    per_pool = tok.shape[0]
    feature_width = width // n_req
    qkv_width = projw.shape[1]
    n_pages, _, page_size, head_width = kv_cache.shape
    slice_width = wout.shape[0]
    rows16 = mask16.shape[0]
    vmem = pl.BlockSpec(memory_space=pltpu.VMEM)
    anywhere = pl.BlockSpec(memory_space=pl.ANY)
    dma = pltpu.SemaphoreType.DMA
    f32 = jnp.float32
    bf16 = jnp.bfloat16
    return pl.pallas_call(
        layer_kernel,
        out_shape=jax.ShapeDtypeStruct((owned, width), bf16),
        in_specs=[vmem] * 7 + [anywhere] + [vmem] * 3 + [anywhere, anywhere],
        out_specs=vmem,
        scratch_shapes=[
            pltpu.VMEM((n_req, per_pool, feature_width), bf16),
            pltpu.VMEM((n_req, per_pool, feature_width), bf16),
            pltpu.VMEM((8 * n_req, feature_width), f32),
            pltpu.VMEM((n_req, per_pool, qkv_width), f32),
            pltpu.VMEM((n_req, per_pool, qkv_width), f32),
            pltpu.VMEM((n_pages + 1, page_size, head_width), bf16),
            pltpu.VMEM((n_pages + 1, page_size, head_width), bf16),
            pltpu.VMEM((rows16, head_width), f32),
            pltpu.VMEM((rows16, head_width), f32),
            pltpu.VMEM((rows16, head_width), f32),
            pltpu.VMEM((rows16, head_width), f32),
            pltpu.VMEM((n_req, per_pool, slice_width), bf16),
            pltpu.VMEM((n_req, per_pool, slice_width), bf16),
            pltpu.VMEM((8 * n_req, 128), f32),
            pltpu.VMEM((128, width), bf16),
            pltpu.VMEM((n_wide, owned, width), bf16),
            pltpu.VMEM((n_wide, owned, width), bf16),
            pltpu.VMEM((owned, width), bf16),
            pltpu.VMEM((n_narrow, owned, width), bf16),
            pltpu.VMEM((n_narrow * owned, width), f32),
            pltpu.VMEM((n_narrow * owned, width), f32),
            pltpu.VMEM((n_narrow, owned, width), bf16),
            pltpu.VMEM((n_narrow, owned, width), bf16),
            pltpu.VMEM((wgu.shape[0], wgu.shape[1] * wgu.shape[2]), bf16),
            pltpu.VMEM(wd.shape, bf16),
            pltpu.VMEM(wgu.shape, bf16),
            dma((n_req,)), dma((n_req,)),
            dma((n_req,)), dma((n_req,)),
            dma((n_req,)), dma((n_req,)),
            dma((n_wide,)), dma((n_wide,)),
            dma((n_narrow,)), dma((n_narrow,)),
            dma((n_narrow,)), dma((n_narrow,)),
            dma((4,)),
        ],
        compiler_params=pltpu.CompilerParams(
            collective_id=cid, has_side_effects=True, vmem_limit_bytes=48 * 1024 * 1024
        ),
    )(tok, gains, qk_gains, order_pad, projw, trig, mask16, kv_cache,
      unperm, wout, residual, wgu, wd)

def rms_scale(value_entries, gain_row):
    mean_square = jnp.mean(value_entries * value_entries, axis=-1, keepdims=True)
    return value_entries * lax.rsqrt(mean_square + eps_norm) * gain_row


def rotate(value_entries, position):
    half_width = value_entries.shape[-1] // 2
    frequency = rope_base ** (
        -jnp.arange(half_width, dtype=jnp.float32) * 2.0 / value_entries.shape[-1]
    )
    angles = position[:, None, None] * frequency
    cosines = jnp.cos(angles)
    sines = jnp.sin(angles)
    first_half = value_entries[..., :half_width]
    second_half = value_entries[..., half_width:]
    return jnp.concatenate(
        [first_half * cosines - second_half * sines, second_half * cosines + first_half * sines],
        axis=-1,
    )


def shards(
    tokens,
    gains,
    qk_gains,
    w_query,
    key_value_weight,
    output_weight,
    w_gateup,
    w_down,
    kv_cache,
    lengths,
    page_table,
):
    req_position = lax.axis_index("req")
    kv_position = lax.axis_index("kv")
    hid_position = lax.axis_index("hid")
    req_total = lax.axis_size("req")
    hid_total = lax.axis_size("hid")
    kv_total = lax.axis_size("kv")
    rows_here, _, model_width = tokens.shape
    half_rows = rows_here // kv_total
    head_width = qk_gains.shape[1]
    per_group = w_query.shape[1] // head_width
    pool_size, _, page_size, _ = kv_cache.shape
    request_count = rows_here * req_total
    feature_width = w_query.shape[0]

    own_rows = tokens[:, 0, :]

    group_lengths = lax.dynamic_index_in_dim(lengths, hid_position, axis=1, keepdims=False)
    group_table = lax.dynamic_index_in_dim(page_table, hid_position, axis=1, keepdims=False)
    request_ids = jnp.arange(request_count, dtype=jnp.int32)
    pool_of = (group_table[:, 0] // pool_size) // hid_total
    pool_pos = pool_of * rows_here + request_ids % rows_here
    order = pool_pos[None, :] == request_ids[:, None]
    pad_to = 8 - rows_here
    order_pad = order.reshape(req_total, rows_here, req_total, rows_here)
    order_pad = jnp.pad(order_pad, ((0, 0), (0, pad_to), (0, 0), (0, pad_to)))
    order_pad = order_pad.reshape(8 * req_total, 8 * req_total).astype(jnp.bfloat16)
    unperm = order.T.reshape(request_count, req_total, rows_here)
    unperm = jnp.pad(unperm, ((0, 0), (0, 0), (0, pad_to)))
    unperm = unperm.reshape(request_count, 8 * req_total).astype(jnp.bfloat16)

    projection = jnp.concatenate(
        [w_query, key_value_weight.reshape(key_value_weight.shape[0], -1)], axis=1
    )

    mine = lax.dynamic_slice_in_dim(order, req_position * rows_here, rows_here, 0)
    my_lengths = jnp.sum(jnp.where(mine, group_lengths[None, :], 0), axis=1)
    my_tables = jnp.sum(jnp.where(mine[:, :, None], group_table[None, :, :], 0), axis=1)
    position = my_lengths.astype(jnp.float32)
    half_width = head_width // 2
    frequency = rope_base ** (-jnp.arange(half_width, dtype=jnp.float32) * 2.0 / head_width)
    angles = position[:, None] * frequency
    trig = jnp.stack([jnp.cos(angles), jnp.sin(angles)])

    slot_base = (req_position * hid_total + hid_position) * pool_size
    local = my_tables - slot_base
    slots = jnp.arange(pool_size, dtype=jnp.int32)
    match = local[:, :, None] == slots[None, None, :]
    page_ids = jnp.arange(my_tables.shape[1], dtype=jnp.int32)
    owner_hit = jnp.any(match, axis=1)
    page_of = jnp.sum(jnp.where(match, page_ids[None, :, None], 0), axis=(0, 1))
    cache_pos = page_of[:, None] * page_size + jnp.arange(page_size, dtype=jnp.int32)[None, :]
    live = owner_hit[:, :, None] & (cache_pos[None] < my_lengths[:, None, None])
    live = live.reshape(rows_here, pool_size * page_size)
    live = jnp.pad(live, ((0, 0), (0, page_size)))
    mask16 = jnp.tile(live, (per_group, 1)).astype(jnp.int32)

    residual = lax.dynamic_slice_in_dim(own_rows, kv_position * half_rows, half_rows, 0)
    hidden_width = w_down.shape[0]
    result = layer(
        own_rows,
        gains,
        qk_gains,
        order_pad,
        projection,
        trig,
        mask16,
        kv_cache,
        unperm,
        output_weight[0],
        residual.astype(jnp.float32),
        w_gateup,
        w_down,
        0,
    )
    return result[:, None, :]


def solution(mesh):
    return jax.shard_map(
        shards,
        mesh=mesh,
        in_specs=(
            P("req", "hid", None),
            P(),
            P(),
            P("req", "kv"),
            P("req", None, "kv"),
            P("kv", "req", None),
            P(None, None, ("kv", "hid")),
            P(("kv", "hid"), None),
            P(("req", "hid"), None, None, "kv"),
            P(),
            P(),
        ),
        out_specs=P(("req", "kv"), "hid", None),
        check_vma=False,
    )
```

```python
import functools

import jax
import jax.numpy as jnp
from jax import lax
from jax.experimental import pallas as pl
from jax.experimental.pallas import tpu as pltpu
from jax.sharding import PartitionSpec as P

eps_norm = 1e-06
rope_base = 1000000.0
neg_large = -1e30
MESH = pl.DeviceIdType.MESH
AXES = ("req", "kv", "hid")


def group_layout(group):
    sizes = [lax.axis_size(a) for a in group]
    me = 0
    for a, s in zip(group, sizes):
        me = me * s + lax.axis_index(a)
    total = 1
    for s in sizes:
        total *= s
    return sizes, me, total


def device_of(group, sizes, position):
    coords = {a: lax.axis_index(a) for a in AXES}
    rest = position
    for a, s in reversed(list(zip(group, sizes))):
        coords[a] = rest % s
        rest = rest // s
    return tuple(coords[a] for a in AXES)


def exchange_kernel(group, bcast, x_ref, y_ref, send_sem, recv_sem):
    sizes, me, n = group_layout(group)
    barrier = pltpu.get_barrier_semaphore()
    for s in range(1, n):
        peer = lax.rem(me + s, n)
        pl.semaphore_signal(
            barrier, inc=1, device_id=device_of(group, sizes, peer), device_id_type=MESH
        )
    pl.semaphore_wait(barrier, n - 1)
    copies = []
    for s in range(1, n):
        peer = lax.rem(me + s, n)
        src = x_ref if bcast else x_ref.at[peer]
        copy = pltpu.make_async_remote_copy(
            src_ref=src,
            dst_ref=y_ref.at[me],
            send_sem=send_sem.at[s],
            recv_sem=recv_sem.at[s],
            device_id=device_of(group, sizes, peer),
            device_id_type=MESH,
        )
        copy.start()
        copies.append(copy)
    if bcast:
        y_ref[me] = x_ref[...]
    else:
        y_ref[me] = x_ref[me]
    for s in range(1, n):
        copies[s - 1].wait_send()
        origin = lax.rem(me + n - s, n)
        src = x_ref if bcast else x_ref.at[origin]
        pltpu.make_async_remote_copy(
            src_ref=src,
            dst_ref=y_ref.at[origin],
            send_sem=send_sem.at[s],
            recv_sem=recv_sem.at[s],
            device_id=device_of(group, sizes, origin),
            device_id_type=MESH,
        ).wait_recv()


def exchange(x, group, cid, bcast=False):
    n = 1
    for a in group:
        n *= lax.axis_size(a)
    block = x.shape if bcast else x.shape[1:]
    return pl.pallas_call(
        functools.partial(exchange_kernel, group, bcast),
        out_shape=jax.ShapeDtypeStruct((n,) + tuple(block), x.dtype),
        in_specs=[pl.BlockSpec(memory_space=pltpu.VMEM)],
        out_specs=pl.BlockSpec(memory_space=pltpu.VMEM),
        scratch_shapes=[pltpu.SemaphoreType.DMA((n,)), pltpu.SemaphoreType.DMA((n,))],
        compiler_params=pltpu.CompilerParams(collective_id=cid, has_side_effects=True),
    )(x)


def start_copies(group, src_of, dst_ref, send_sem, recv_sem):
    sizes, me, n = group_layout(group)
    copies = []
    for s in range(1, n):
        peer = lax.rem(me + s, n)
        copy = pltpu.make_async_remote_copy(
            src_ref=src_of(peer),
            dst_ref=dst_ref.at[me],
            send_sem=send_sem.at[s],
            recv_sem=recv_sem.at[s],
            device_id=device_of(group, sizes, peer),
            device_id_type=MESH,
        )
        copy.start()
        copies.append(copy)

    def finish():
        for s in range(1, n):
            copies[s - 1].wait_send()
            origin = lax.rem(me + n - s, n)
            pltpu.make_async_remote_copy(
                src_ref=src_of(origin),
                dst_ref=dst_ref.at[origin],
                send_sem=send_sem.at[s],
                recv_sem=recv_sem.at[s],
                device_id=device_of(group, sizes, origin),
                device_id_type=MESH,
            ).wait_recv()

    return me, finish


def rms_rows(value_entries, gain_row):
    mean_square = jnp.mean(value_entries * value_entries, axis=-1, keepdims=True)
    return value_entries * lax.rsqrt(mean_square + eps_norm) * gain_row


def unpack_rows(wgu_raw, wgu_v, start, count):
    hidden_width = wgu_raw.shape[2]
    rows = pl.ds(start, count)
    wgu_v[rows, 0:hidden_width] = wgu_raw[rows, 0, :]
    wgu_v[rows, hidden_width:] = wgu_raw[rows, 1, :]


def layer_kernel(
    tok_ref, gains_ref, qkg_ref, order_ref, projw_ref, trig_ref, mask_ref, kv_hbm,
    unperm_ref, wout_ref, resid_ref, wgu_hbm, wd_hbm,
    out_ref,
    tok_src, y_tok, tok_rows, send_qkv, y_qkv, keys_v, vals_v, q16, k16, v16, comb,
    send_att, y_att, att_rows, w_pad, send_proj, y_proj, ffn_src, y_ffn, ffn_rows, ffn_out,
    send_red, y_red, wgu_v, wd_v, wgu_raw,
    tok_send, tok_recv, qkv_send, qkv_recv,
    att_send, att_recv, proj_send, proj_recv, ffn_send, ffn_recv, red_send, red_recv, w_sem,
):
    n_pages = kv_hbm.shape[0]
    keys_copy = pltpu.make_async_copy(kv_hbm.at[:, 0], keys_v.at[pl.ds(0, n_pages)], w_sem.at[0])
    vals_copy = pltpu.make_async_copy(kv_hbm.at[:, 1], vals_v.at[pl.ds(0, n_pages)], w_sem.at[1])
    wgu_copy = pltpu.make_async_copy(wgu_hbm, wgu_raw, w_sem.at[2])
    wd_copy = pltpu.make_async_copy(wd_hbm, wd_v, w_sem.at[3])
    keys_copy.start()
    vals_copy.start()
    wgu_copy.start()
    wd_copy.start()

    wide = ("req", "kv")
    narrow = ("kv", "hid")
    wide_sizes, wide_me, wide_n = group_layout(wide)
    narrow_sizes, narrow_me, narrow_n = group_layout(narrow)
    half = narrow_n // 2
    barrier = pltpu.get_barrier_semaphore()
    for s in range(1, wide_n):
        peer = lax.rem(wide_me + s, wide_n)
        pl.semaphore_signal(
            barrier, inc=1, device_id=device_of(wide, wide_sizes, peer), device_id_type=MESH
        )
    for s in range(1, narrow_n):
        if s == half:
            continue
        peer = lax.rem(narrow_me + s, narrow_n)
        pl.semaphore_signal(
            barrier, inc=1, device_id=device_of(narrow, narrow_sizes, peer), device_id_type=MESH
        )

    n_req, per_pool, feature_width = tok_src.shape
    normed = rms_rows(tok_ref[...].astype(jnp.float32), gains_ref[0:1, :]).astype(jnp.bfloat16)
    for k in range(n_req):
        tok_src[k] = normed[:, feature_width * k : feature_width * (k + 1)]
    tok_rows[...] = jnp.zeros_like(tok_rows)
    pl.semaphore_wait(barrier, wide_n - 1 + narrow_n - 2)

    tok_me, tok_finish = start_copies(("req",), lambda k: tok_src.at[k], y_tok, tok_send, tok_recv)
    y_tok[tok_me] = tok_src[tok_me]
    wgu_copy.wait()
    unpack_rows(wgu_raw, wgu_v, 0, 512)
    tok_finish()
    for k in range(n_req):
        tok_rows[8 * k : 8 * k + per_pool, :] = y_tok[k].astype(jnp.float32)
    pooled = jnp.dot(
        order_ref[...], tok_rows[...].astype(jnp.bfloat16), preferred_element_type=jnp.float32
    ).astype(jnp.bfloat16)
    partial = jnp.dot(pooled, projw_ref[...], preferred_element_type=jnp.float32)
    for k in range(n_req):
        send_qkv[k] = partial[8 * k : 8 * k + per_pool]

    qkv_me, qkv_finish = start_copies(("req",), lambda k: send_qkv.at[k], y_qkv, qkv_send, qkv_recv)
    y_qkv[qkv_me] = send_qkv[qkv_me]
    unpack_rows(wgu_raw, wgu_v, 512, 512)
    qkv_finish()
    summed = y_qkv[0]
    for k in range(1, n_req):
        summed = summed + y_qkv[k]
    cosines = trig_ref[0]
    sines = trig_ref[1]
    head_width = q16.shape[1]
    half_width = head_width // 2

    def rot(v):
        a = v[:, :half_width]
        b = v[:, half_width:]
        return jnp.concatenate([a * cosines - b * sines, b * cosines + a * sines], axis=-1)

    per_group = q16.shape[0] // per_pool
    for h in range(per_group):
        qh = rot(rms_rows(summed[:, head_width * h : head_width * (h + 1)], qkg_ref[0:1, :]))
        q16[per_pool * h : per_pool * (h + 1), :] = qh.astype(jnp.bfloat16).astype(jnp.float32)
    split_at = per_group * head_width
    kn = rot(rms_rows(summed[:, split_at : split_at + head_width], qkg_ref[1:2, :]))
    kn = kn.astype(jnp.bfloat16).astype(jnp.float32)
    vn = rms_rows(summed[:, split_at + head_width :], 1.0)
    vn = vn.astype(jnp.bfloat16).astype(jnp.float32)
    for h in range(per_group):
        k16[per_pool * h : per_pool * (h + 1), :] = kn
        v16[per_pool * h : per_pool * (h + 1), :] = vn

    keys_copy.wait()
    vals_copy.wait()
    keys_v[n_pages] = jnp.zeros(keys_v.shape[1:], keys_v.dtype)
    vals_v[n_pages] = jnp.zeros(vals_v.shape[1:], vals_v.dtype)
    total_pos = keys_v.shape[0] * keys_v.shape[1]
    keys = keys_v[...].reshape(total_pos, head_width)
    vals = vals_v[...].reshape(total_pos, head_width)
    scale_factor = head_width ** (-0.5)
    q_f = q16[...]
    scores = lax.dot_general(
        q_f.astype(jnp.bfloat16), keys, (((1,), (1,)), ((), ())),
        preferred_element_type=jnp.float32,
    ) * scale_factor
    live = mask_ref[...] != 0
    masked = jnp.where(live, scores, neg_large)
    highest_cached = jnp.max(masked, axis=1, keepdims=True)
    weights = jnp.where(live, jnp.exp(masked - highest_cached), 0.0)
    totals = jnp.sum(weights, axis=1, keepdims=True)
    weighted = jnp.dot(weights.astype(jnp.bfloat16), vals, preferred_element_type=jnp.float32)
    own_score = jnp.sum(q_f * k16[...], axis=1, keepdims=True) * scale_factor
    highest = jnp.maximum(highest_cached, own_score)
    old_scale = jnp.exp(highest_cached - highest)
    new_scale = jnp.exp(own_score - highest)
    combined = (weighted * old_scale + new_scale * v16[...]) / (totals * old_scale + new_scale)
    comb[...] = combined.astype(jnp.bfloat16).astype(jnp.float32)
    slice_width = send_att.shape[2]
    per_head = head_width // slice_width
    for k in range(n_req):
        h, m = divmod(k, per_head)
        send_att[k] = comb[per_pool * h : per_pool * (h + 1), slice_width * m : slice_width * (m + 1)].astype(jnp.bfloat16)

    att_me, att_finish = start_copies(("req",), lambda k: send_att.at[k], y_att, att_send, att_recv)
    y_att[att_me] = send_att[att_me]
    att_rows[...] = jnp.zeros_like(att_rows)
    w_pad[...] = jnp.zeros_like(w_pad)
    rows_w = wout_ref.shape[0]
    w_pad[0:rows_w, :] = wout_ref[...]
    unpack_rows(wgu_raw, wgu_v, 1024, 512)
    att_finish()
    for k in range(n_req):
        att_rows[8 * k : 8 * k + per_pool, 0:slice_width] = y_att[k].astype(jnp.float32)
    att_nat = jnp.dot(
        unperm_ref[...], att_rows[...].astype(jnp.bfloat16), preferred_element_type=jnp.float32
    ).astype(jnp.bfloat16)
    proj = jnp.dot(att_nat, w_pad[...], preferred_element_type=jnp.float32)
    n_wide, owned, width = send_proj.shape
    for q in range(n_wide):
        send_proj[q] = proj[owned * q : owned * (q + 1)].astype(jnp.bfloat16)

    proj_me, proj_finish = start_copies(wide, lambda k: send_proj.at[k], y_proj, proj_send, proj_recv)
    y_proj[proj_me] = send_proj[proj_me]
    unpack_rows(wgu_raw, wgu_v, 1536, 512)
    proj_finish()
    projected = y_proj[0].astype(jnp.float32)
    for k in range(1, n_wide):
        projected = projected + y_proj[k].astype(jnp.float32)
    middle = (resid_ref[...] + rms_rows(projected, gains_ref[1:2, :])).astype(jnp.bfloat16)
    ffn_src[...] = rms_rows(middle.astype(jnp.float32), gains_ref[2:3, :]).astype(jnp.bfloat16)

    ffn_me, ffn_finish = start_copies(narrow, lambda k: ffn_src, y_ffn, ffn_send, ffn_recv)
    y_ffn[ffn_me] = ffn_src[...]
    ffn_finish()
    for k in range(narrow_n):
        ffn_rows[owned * k : owned * (k + 1), :] = y_ffn[k].astype(jnp.float32)
    wd_copy.wait()
    gate_up = jnp.dot(
        ffn_rows[...].astype(jnp.bfloat16), wgu_v[...], preferred_element_type=jnp.float32
    )
    hidden_width = wd_v.shape[0]
    hidden = (
        jax.nn.gelu(gate_up[:, :hidden_width], approximate=True) * gate_up[:, hidden_width:]
    ).astype(jnp.bfloat16)
    ffn_out[...] = jnp.dot(hidden, wd_v[...], preferred_element_type=jnp.float32)
    for k in range(narrow_n):
        send_red[k] = ffn_out[owned * k : owned * (k + 1), :].astype(jnp.bfloat16)

    red_me, red_finish = start_copies(narrow, lambda k: send_red.at[k], y_red, red_send, red_recv)
    y_red[red_me] = send_red[red_me]
    red_finish()
    ffn_sum = y_red[0].astype(jnp.float32)
    for k in range(1, narrow_n):
        ffn_sum = ffn_sum + y_red[k].astype(jnp.float32)
    out_ref[...] = (middle.astype(jnp.float32) + rms_rows(ffn_sum, gains_ref[3:4, :])).astype(
        out_ref.dtype
    )


def layer(tok, gains, qk_gains, order_pad, projw, trig, mask16, kv_cache,
          unperm, wout, residual, wgu, wd, cid):
    n_req = lax.axis_size("req")
    n_wide = n_req * lax.axis_size("kv")
    n_narrow = lax.axis_size("kv") * lax.axis_size("hid")
    owned, width = residual.shape
    per_pool = tok.shape[0]
    feature_width = width // n_req
    qkv_width = projw.shape[1]
    n_pages, _, page_size, head_width = kv_cache.shape
    slice_width = wout.shape[0]
    rows16 = mask16.shape[0]
    vmem = pl.BlockSpec(memory_space=pltpu.VMEM)
    anywhere = pl.BlockSpec(memory_space=pl.ANY)
    dma = pltpu.SemaphoreType.DMA
    f32 = jnp.float32
    bf16 = jnp.bfloat16
    return pl.pallas_call(
        layer_kernel,
        out_shape=jax.ShapeDtypeStruct((owned, width), bf16),
        in_specs=[vmem] * 7 + [anywhere] + [vmem] * 3 + [anywhere, anywhere],
        out_specs=vmem,
        scratch_shapes=[
            pltpu.VMEM((n_req, per_pool, feature_width), bf16),
            pltpu.VMEM((n_req, per_pool, feature_width), bf16),
            pltpu.VMEM((8 * n_req, feature_width), f32),
            pltpu.VMEM((n_req, per_pool, qkv_width), f32),
            pltpu.VMEM((n_req, per_pool, qkv_width), f32),
            pltpu.VMEM((n_pages + 1, page_size, head_width), bf16),
            pltpu.VMEM((n_pages + 1, page_size, head_width), bf16),
            pltpu.VMEM((rows16, head_width), f32),
            pltpu.VMEM((rows16, head_width), f32),
            pltpu.VMEM((rows16, head_width), f32),
            pltpu.VMEM((rows16, head_width), f32),
            pltpu.VMEM((n_req, per_pool, slice_width), bf16),
            pltpu.VMEM((n_req, per_pool, slice_width), bf16),
            pltpu.VMEM((8 * n_req, 128), f32),
            pltpu.VMEM((128, width), bf16),
            pltpu.VMEM((n_wide, owned, width), bf16),
            pltpu.VMEM((n_wide, owned, width), bf16),
            pltpu.VMEM((owned, width), bf16),
            pltpu.VMEM((n_narrow, owned, width), bf16),
            pltpu.VMEM((n_narrow * owned, width), f32),
            pltpu.VMEM((n_narrow * owned, width), f32),
            pltpu.VMEM((n_narrow, owned, width), bf16),
            pltpu.VMEM((n_narrow, owned, width), bf16),
            pltpu.VMEM((wgu.shape[0], wgu.shape[1] * wgu.shape[2]), bf16),
            pltpu.VMEM(wd.shape, bf16),
            pltpu.VMEM(wgu.shape, bf16),
            dma((n_req,)), dma((n_req,)),
            dma((n_req,)), dma((n_req,)),
            dma((n_req,)), dma((n_req,)),
            dma((n_wide,)), dma((n_wide,)),
            dma((n_narrow,)), dma((n_narrow,)),
            dma((n_narrow,)), dma((n_narrow,)),
            dma((4,)),
        ],
        compiler_params=pltpu.CompilerParams(
            collective_id=cid, has_side_effects=True
        ),
    )(tok, gains, qk_gains, order_pad, projw, trig, mask16, kv_cache,
      unperm, wout, residual, wgu, wd)

def rms_scale(value_entries, gain_row):
    mean_square = jnp.mean(value_entries * value_entries, axis=-1, keepdims=True)
    return value_entries * lax.rsqrt(mean_square + eps_norm) * gain_row


def rotate(value_entries, position):
    half_width = value_entries.shape[-1] // 2
    frequency = rope_base ** (
        -jnp.arange(half_width, dtype=jnp.float32) * 2.0 / value_entries.shape[-1]
    )
    angles = position[:, None, None] * frequency
    cosines = jnp.cos(angles)
    sines = jnp.sin(angles)
    first_half = value_entries[..., :half_width]
    second_half = value_entries[..., half_width:]
    return jnp.concatenate(
        [first_half * cosines - second_half * sines, second_half * cosines + first_half * sines],
        axis=-1,
    )


def shards(
    tokens,
    gains,
    qk_gains,
    w_query,
    key_value_weight,
    output_weight,
    w_gateup,
    w_down,
    kv_cache,
    lengths,
    page_table,
):
    req_position = lax.axis_index("req")
    kv_position = lax.axis_index("kv")
    hid_position = lax.axis_index("hid")
    req_total = lax.axis_size("req")
    hid_total = lax.axis_size("hid")
    kv_total = lax.axis_size("kv")
    rows_here, _, model_width = tokens.shape
    half_rows = rows_here // kv_total
    head_width = qk_gains.shape[1]
    per_group = w_query.shape[1] // head_width
    pool_size, _, page_size, _ = kv_cache.shape
    request_count = rows_here * req_total
    feature_width = w_query.shape[0]

    own_rows = tokens[:, 0, :]

    group_lengths = lax.dynamic_index_in_dim(lengths, hid_position, axis=1, keepdims=False)
    group_table = lax.dynamic_index_in_dim(page_table, hid_position, axis=1, keepdims=False)
    request_ids = jnp.arange(request_count, dtype=jnp.int32)
    pool_of = (group_table[:, 0] // pool_size) // hid_total
    pool_pos = pool_of * rows_here + request_ids % rows_here
    order = pool_pos[None, :] == request_ids[:, None]
    pad_to = 8 - rows_here
    order_pad = order.reshape(req_total, rows_here, req_total, rows_here)
    order_pad = jnp.pad(order_pad, ((0, 0), (0, pad_to), (0, 0), (0, pad_to)))
    order_pad = order_pad.reshape(8 * req_total, 8 * req_total).astype(jnp.bfloat16)
    unperm = order.T.reshape(request_count, req_total, rows_here)
    unperm = jnp.pad(unperm, ((0, 0), (0, 0), (0, pad_to)))
    unperm = unperm.reshape(request_count, 8 * req_total).astype(jnp.bfloat16)

    projection = jnp.concatenate(
        [w_query, key_value_weight.reshape(key_value_weight.shape[0], -1)], axis=1
    )

    mine = lax.dynamic_slice_in_dim(order, req_position * rows_here, rows_here, 0)
    my_lengths = jnp.sum(jnp.where(mine, group_lengths[None, :], 0), axis=1)
    my_tables = jnp.sum(jnp.where(mine[:, :, None], group_table[None, :, :], 0), axis=1)
    position = my_lengths.astype(jnp.float32)
    half_width = head_width // 2
    frequency = rope_base ** (-jnp.arange(half_width, dtype=jnp.float32) * 2.0 / head_width)
    angles = position[:, None] * frequency
    trig = jnp.stack([jnp.cos(angles), jnp.sin(angles)])

    slot_base = (req_position * hid_total + hid_position) * pool_size
    local = my_tables - slot_base
    slots = jnp.arange(pool_size, dtype=jnp.int32)
    match = local[:, :, None] == slots[None, None, :]
    page_ids = jnp.arange(my_tables.shape[1], dtype=jnp.int32)
    owner_hit = jnp.any(match, axis=1)
    page_of = jnp.sum(jnp.where(match, page_ids[None, :, None], 0), axis=(0, 1))
    cache_pos = page_of[:, None] * page_size + jnp.arange(page_size, dtype=jnp.int32)[None, :]
    live = owner_hit[:, :, None] & (cache_pos[None] < my_lengths[:, None, None])
    live = live.reshape(rows_here, pool_size * page_size)
    live = jnp.pad(live, ((0, 0), (0, page_size)))
    mask16 = jnp.tile(live, (per_group, 1)).astype(jnp.int32)

    residual = lax.dynamic_slice_in_dim(own_rows, kv_position * half_rows, half_rows, 0)
    hidden_width = w_down.shape[0]
    result = layer(
        own_rows,
        gains,
        qk_gains,
        order_pad,
        projection,
        trig,
        mask16,
        kv_cache,
        unperm,
        output_weight[0],
        residual.astype(jnp.float32),
        w_gateup,
        w_down,
        0,
    )
    return result[:, None, :]


def solution(mesh):
    return jax.shard_map(
        shards,
        mesh=mesh,
        in_specs=(
            P("req", "hid", None),
            P(),
            P(),
            P("req", "kv"),
            P("req", None, "kv"),
            P("kv", "req", None),
            P(None, None, ("kv", "hid")),
            P(("kv", "hid"), None),
            P(("req", "hid"), None, None, "kv"),
            P(),
            P(),
        ),
        out_specs=P(("req", "kv"), "hid", None),
        check_vma=False,
    )
```

```python
import functools

import jax
import jax.numpy as jnp
from jax import lax
from jax.experimental import pallas as pl
from jax.experimental.pallas import tpu as pltpu
from jax.sharding import PartitionSpec as P

eps_norm = 1e-06
rope_base = 1000000.0
neg_large = -1e30
MESH = pl.DeviceIdType.MESH
AXES = ("req", "kv", "hid")


def group_layout(group):
    sizes = [lax.axis_size(a) for a in group]
    me = 0
    for a, s in zip(group, sizes):
        me = me * s + lax.axis_index(a)
    total = 1
    for s in sizes:
        total *= s
    return sizes, me, total


def device_of(group, sizes, position):
    coords = {a: lax.axis_index(a) for a in AXES}
    rest = position
    for a, s in reversed(list(zip(group, sizes))):
        coords[a] = rest % s
        rest = rest // s
    return tuple(coords[a] for a in AXES)


def exchange_kernel(group, bcast, x_ref, y_ref, send_sem, recv_sem):
    sizes, me, n = group_layout(group)
    barrier = pltpu.get_barrier_semaphore()
    for s in range(1, n):
        peer = lax.rem(me + s, n)
        pl.semaphore_signal(
            barrier, inc=1, device_id=device_of(group, sizes, peer), device_id_type=MESH
        )
    pl.semaphore_wait(barrier, n - 1)
    copies = []
    for s in range(1, n):
        peer = lax.rem(me + s, n)
        src = x_ref if bcast else x_ref.at[peer]
        copy = pltpu.make_async_remote_copy(
            src_ref=src,
            dst_ref=y_ref.at[me],
            send_sem=send_sem.at[s],
            recv_sem=recv_sem.at[s],
            device_id=device_of(group, sizes, peer),
            device_id_type=MESH,
        )
        copy.start()
        copies.append(copy)
    if bcast:
        y_ref[me] = x_ref[...]
    else:
        y_ref[me] = x_ref[me]
    for s in range(1, n):
        copies[s - 1].wait_send()
        origin = lax.rem(me + n - s, n)
        src = x_ref if bcast else x_ref.at[origin]
        pltpu.make_async_remote_copy(
            src_ref=src,
            dst_ref=y_ref.at[origin],
            send_sem=send_sem.at[s],
            recv_sem=recv_sem.at[s],
            device_id=device_of(group, sizes, origin),
            device_id_type=MESH,
        ).wait_recv()


def exchange(x, group, cid, bcast=False):
    n = 1
    for a in group:
        n *= lax.axis_size(a)
    block = x.shape if bcast else x.shape[1:]
    return pl.pallas_call(
        functools.partial(exchange_kernel, group, bcast),
        out_shape=jax.ShapeDtypeStruct((n,) + tuple(block), x.dtype),
        in_specs=[pl.BlockSpec(memory_space=pltpu.VMEM)],
        out_specs=pl.BlockSpec(memory_space=pltpu.VMEM),
        scratch_shapes=[pltpu.SemaphoreType.DMA((n,)), pltpu.SemaphoreType.DMA((n,))],
        compiler_params=pltpu.CompilerParams(collective_id=cid, has_side_effects=True),
    )(x)


def start_copies(group, src_of, dst_ref, send_sem, recv_sem):
    sizes, me, n = group_layout(group)
    copies = []
    for s in range(1, n):
        peer = lax.rem(me + s, n)
        copy = pltpu.make_async_remote_copy(
            src_ref=src_of(peer),
            dst_ref=dst_ref.at[me],
            send_sem=send_sem.at[s],
            recv_sem=recv_sem.at[s],
            device_id=device_of(group, sizes, peer),
            device_id_type=MESH,
        )
        copy.start()
        copies.append(copy)

    def finish():
        for s in range(1, n):
            copies[s - 1].wait_send()
            origin = lax.rem(me + n - s, n)
            pltpu.make_async_remote_copy(
                src_ref=src_of(origin),
                dst_ref=dst_ref.at[origin],
                send_sem=send_sem.at[s],
                recv_sem=recv_sem.at[s],
                device_id=device_of(group, sizes, origin),
                device_id_type=MESH,
            ).wait_recv()

    return me, finish


def rms_rows(value_entries, gain_row):
    mean_square = jnp.mean(value_entries * value_entries, axis=-1, keepdims=True)
    return value_entries * lax.rsqrt(mean_square + eps_norm) * gain_row


def unpack_rows(wgu_raw, wgu_v, start, count):
    hidden_width = wgu_raw.shape[2]
    rows = pl.ds(start, count)
    wgu_v[rows, 0:hidden_width] = wgu_raw[rows, 0, :]
    wgu_v[rows, hidden_width:] = wgu_raw[rows, 1, :]


def layer_kernel(
    tok_ref, gains_ref, qkg_ref, order_ref, wq_ref, kvw_ref, trig_ref, mask_ref, kv_hbm,
    unperm_ref, wout_ref, wgu_hbm, wd_hbm,
    out_ref,
    tok_src, y_tok, tok_rows, send_qkv, y_qkv, keys_v, vals_v, q16, k16, v16, comb,
    send_att, y_att, att_rows, w_pad, send_proj, y_proj, ffn_src, y_ffn, ffn_rows, ffn_out,
    send_red, y_red, wgu_v, wd_v, wgu_raw, kv_v,
    tok_send, tok_recv, qkv_send, qkv_recv,
    att_send, att_recv, proj_send, proj_recv, ffn_send, ffn_recv, red_send, red_recv, w_sem,
):
    n_pages = kv_hbm.shape[0]
    keys_copy = pltpu.make_async_copy(kv_hbm.at[:, 0], keys_v.at[pl.ds(0, n_pages)], w_sem.at[0])
    vals_copy = pltpu.make_async_copy(kv_hbm.at[:, 1], vals_v.at[pl.ds(0, n_pages)], w_sem.at[1])
    wgu_copy = pltpu.make_async_copy(wgu_hbm, wgu_raw, w_sem.at[2])
    wd_copy = pltpu.make_async_copy(wd_hbm, wd_v, w_sem.at[3])
    keys_copy.start()
    vals_copy.start()
    wgu_copy.start()
    wd_copy.start()

    wide = ("req", "kv")
    narrow = ("kv", "hid")
    wide_sizes, wide_me, wide_n = group_layout(wide)
    narrow_sizes, narrow_me, narrow_n = group_layout(narrow)
    half = narrow_n // 2
    barrier = pltpu.get_barrier_semaphore()
    for s in range(1, wide_n):
        peer = lax.rem(wide_me + s, wide_n)
        pl.semaphore_signal(
            barrier, inc=1, device_id=device_of(wide, wide_sizes, peer), device_id_type=MESH
        )
    for s in range(1, narrow_n):
        if s == half:
            continue
        peer = lax.rem(narrow_me + s, narrow_n)
        pl.semaphore_signal(
            barrier, inc=1, device_id=device_of(narrow, narrow_sizes, peer), device_id_type=MESH
        )

    n_req, per_pool, feature_width = tok_src.shape
    normed = rms_rows(tok_ref[...].astype(jnp.float32), gains_ref[0:1, :]).astype(jnp.bfloat16)
    for k in range(n_req):
        tok_src[k] = normed[:, feature_width * k : feature_width * (k + 1)]
    tok_rows[...] = jnp.zeros_like(tok_rows)
    kv_half = kvw_ref.shape[2]
    kv_v[:, 0:kv_half] = kvw_ref[:, 0, :]
    kv_v[:, kv_half:] = kvw_ref[:, 1, :]
    pl.semaphore_wait(barrier, wide_n - 1 + narrow_n - 2)

    tok_me, tok_finish = start_copies(("req",), lambda k: tok_src.at[k], y_tok, tok_send, tok_recv)
    y_tok[tok_me] = tok_src[tok_me]
    wgu_copy.wait()
    unpack_rows(wgu_raw, wgu_v, 0, 512)
    tok_finish()
    for k in range(n_req):
        tok_rows[8 * k : 8 * k + per_pool, :] = y_tok[k].astype(jnp.float32)
    pooled = jnp.dot(
        order_ref[...], tok_rows[...].astype(jnp.bfloat16), preferred_element_type=jnp.float32
    ).astype(jnp.bfloat16)
    q_width = wq_ref.shape[1]
    partial_q = jnp.dot(pooled, wq_ref[...], preferred_element_type=jnp.float32)
    partial_kv = jnp.dot(pooled, kv_v[...], preferred_element_type=jnp.float32)
    for k in range(n_req):
        send_qkv[k, :, 0:q_width] = partial_q[8 * k : 8 * k + per_pool]
        send_qkv[k, :, q_width:] = partial_kv[8 * k : 8 * k + per_pool]

    qkv_me, qkv_finish = start_copies(("req",), lambda k: send_qkv.at[k], y_qkv, qkv_send, qkv_recv)
    y_qkv[qkv_me] = send_qkv[qkv_me]
    unpack_rows(wgu_raw, wgu_v, 512, 512)
    qkv_finish()
    summed = y_qkv[0]
    for k in range(1, n_req):
        summed = summed + y_qkv[k]
    cosines = trig_ref[0]
    sines = trig_ref[1]
    head_width = q16.shape[1]
    half_width = head_width // 2

    def rot(v):
        a = v[:, :half_width]
        b = v[:, half_width:]
        return jnp.concatenate([a * cosines - b * sines, b * cosines + a * sines], axis=-1)

    per_group = q16.shape[0] // per_pool
    for h in range(per_group):
        qh = rot(rms_rows(summed[:, head_width * h : head_width * (h + 1)], qkg_ref[0:1, :]))
        q16[per_pool * h : per_pool * (h + 1), :] = qh.astype(jnp.bfloat16).astype(jnp.float32)
    split_at = per_group * head_width
    kn = rot(rms_rows(summed[:, split_at : split_at + head_width], qkg_ref[1:2, :]))
    kn = kn.astype(jnp.bfloat16).astype(jnp.float32)
    vn = rms_rows(summed[:, split_at + head_width :], 1.0)
    vn = vn.astype(jnp.bfloat16).astype(jnp.float32)
    for h in range(per_group):
        k16[per_pool * h : per_pool * (h + 1), :] = kn
        v16[per_pool * h : per_pool * (h + 1), :] = vn

    keys_copy.wait()
    vals_copy.wait()
    keys_v[n_pages] = jnp.zeros(keys_v.shape[1:], keys_v.dtype)
    vals_v[n_pages] = jnp.zeros(vals_v.shape[1:], vals_v.dtype)
    total_pos = keys_v.shape[0] * keys_v.shape[1]
    keys = keys_v[...].reshape(total_pos, head_width)
    vals = vals_v[...].reshape(total_pos, head_width)
    scale_factor = head_width ** (-0.5)
    q_f = q16[...]
    scores = lax.dot_general(
        q_f.astype(jnp.bfloat16), keys, (((1,), (1,)), ((), ())),
        preferred_element_type=jnp.float32,
    ) * scale_factor
    live = mask_ref[...] != 0
    masked = jnp.where(live, scores, neg_large)
    highest_cached = jnp.max(masked, axis=1, keepdims=True)
    weights = jnp.where(live, jnp.exp(masked - highest_cached), 0.0)
    totals = jnp.sum(weights, axis=1, keepdims=True)
    weighted = jnp.dot(weights.astype(jnp.bfloat16), vals, preferred_element_type=jnp.float32)
    own_score = jnp.sum(q_f * k16[...], axis=1, keepdims=True) * scale_factor
    highest = jnp.maximum(highest_cached, own_score)
    old_scale = jnp.exp(highest_cached - highest)
    new_scale = jnp.exp(own_score - highest)
    combined = (weighted * old_scale + new_scale * v16[...]) / (totals * old_scale + new_scale)
    comb[...] = combined.astype(jnp.bfloat16).astype(jnp.float32)
    slice_width = send_att.shape[2]
    per_head = head_width // slice_width
    for k in range(n_req):
        h, m = divmod(k, per_head)
        send_att[k] = comb[per_pool * h : per_pool * (h + 1), slice_width * m : slice_width * (m + 1)].astype(jnp.bfloat16)

    att_me, att_finish = start_copies(("req",), lambda k: send_att.at[k], y_att, att_send, att_recv)
    y_att[att_me] = send_att[att_me]
    att_rows[...] = jnp.zeros_like(att_rows)
    w_pad[...] = jnp.zeros_like(w_pad)
    rows_w = wout_ref.shape[0]
    w_pad[0:rows_w, :] = wout_ref[...]
    unpack_rows(wgu_raw, wgu_v, 1024, 512)
    att_finish()
    for k in range(n_req):
        att_rows[8 * k : 8 * k + per_pool, 0:slice_width] = y_att[k].astype(jnp.float32)
    att_nat = jnp.dot(
        unperm_ref[...], att_rows[...].astype(jnp.bfloat16), preferred_element_type=jnp.float32
    ).astype(jnp.bfloat16)
    proj = jnp.dot(att_nat, w_pad[...], preferred_element_type=jnp.float32)
    n_wide, owned, width = send_proj.shape
    for q in range(n_wide):
        send_proj[q] = proj[owned * q : owned * (q + 1)].astype(jnp.bfloat16)

    proj_me, proj_finish = start_copies(wide, lambda k: send_proj.at[k], y_proj, proj_send, proj_recv)
    y_proj[proj_me] = send_proj[proj_me]
    unpack_rows(wgu_raw, wgu_v, 1536, 512)
    proj_finish()
    projected = y_proj[0].astype(jnp.float32)
    for k in range(1, n_wide):
        projected = projected + y_proj[k].astype(jnp.float32)
    own = tok_ref[...].astype(jnp.float32)
    residual = jnp.where(lax.axis_index("kv") == 0, own[0:owned], own[owned : 2 * owned])
    middle = (residual + rms_rows(projected, gains_ref[1:2, :])).astype(jnp.bfloat16)
    ffn_src[...] = rms_rows(middle.astype(jnp.float32), gains_ref[2:3, :]).astype(jnp.bfloat16)

    ffn_me, ffn_finish = start_copies(narrow, lambda k: ffn_src, y_ffn, ffn_send, ffn_recv)
    y_ffn[ffn_me] = ffn_src[...]
    ffn_finish()
    for k in range(narrow_n):
        ffn_rows[owned * k : owned * (k + 1), :] = y_ffn[k].astype(jnp.float32)
    wd_copy.wait()
    gate_up = jnp.dot(
        ffn_rows[...].astype(jnp.bfloat16), wgu_v[...], preferred_element_type=jnp.float32
    )
    hidden_width = wd_v.shape[0]
    hidden = (
        jax.nn.gelu(gate_up[:, :hidden_width], approximate=True) * gate_up[:, hidden_width:]
    ).astype(jnp.bfloat16)
    ffn_out[...] = jnp.dot(hidden, wd_v[...], preferred_element_type=jnp.float32)
    for k in range(narrow_n):
        send_red[k] = ffn_out[owned * k : owned * (k + 1), :].astype(jnp.bfloat16)

    red_me, red_finish = start_copies(narrow, lambda k: send_red.at[k], y_red, red_send, red_recv)
    y_red[red_me] = send_red[red_me]
    red_finish()
    ffn_sum = y_red[0].astype(jnp.float32)
    for k in range(1, narrow_n):
        ffn_sum = ffn_sum + y_red[k].astype(jnp.float32)
    out_ref[...] = (middle.astype(jnp.float32) + rms_rows(ffn_sum, gains_ref[3:4, :])).astype(
        out_ref.dtype
    )


def layer(tok, gains, qk_gains, order_pad, wq, kvw, trig, mask16, kv_cache,
          unperm, wout, wgu, wd, cid):
    n_req = lax.axis_size("req")
    n_wide = n_req * lax.axis_size("kv")
    n_narrow = lax.axis_size("kv") * lax.axis_size("hid")
    per_pool, width = tok.shape
    owned = per_pool // lax.axis_size("kv")
    feature_width = width // n_req
    qkv_width = wq.shape[1] + kvw.shape[1] * kvw.shape[2]
    n_pages, _, page_size, head_width = kv_cache.shape
    slice_width = wout.shape[0]
    rows16 = mask16.shape[0]
    vmem = pl.BlockSpec(memory_space=pltpu.VMEM)
    anywhere = pl.BlockSpec(memory_space=pl.ANY)
    dma = pltpu.SemaphoreType.DMA
    f32 = jnp.float32
    bf16 = jnp.bfloat16
    return pl.pallas_call(
        layer_kernel,
        out_shape=jax.ShapeDtypeStruct((owned, width), bf16),
        in_specs=[vmem] * 8 + [anywhere] + [vmem] * 2 + [anywhere, anywhere],
        out_specs=vmem,
        scratch_shapes=[
            pltpu.VMEM((n_req, per_pool, feature_width), bf16),
            pltpu.VMEM((n_req, per_pool, feature_width), bf16),
            pltpu.VMEM((8 * n_req, feature_width), f32),
            pltpu.VMEM((n_req, per_pool, qkv_width), f32),
            pltpu.VMEM((n_req, per_pool, qkv_width), f32),
            pltpu.VMEM((n_pages + 1, page_size, head_width), bf16),
            pltpu.VMEM((n_pages + 1, page_size, head_width), bf16),
            pltpu.VMEM((rows16, head_width), f32),
            pltpu.VMEM((rows16, head_width), f32),
            pltpu.VMEM((rows16, head_width), f32),
            pltpu.VMEM((rows16, head_width), f32),
            pltpu.VMEM((n_req, per_pool, slice_width), bf16),
            pltpu.VMEM((n_req, per_pool, slice_width), bf16),
            pltpu.VMEM((8 * n_req, 128), f32),
            pltpu.VMEM((128, width), bf16),
            pltpu.VMEM((n_wide, owned, width), bf16),
            pltpu.VMEM((n_wide, owned, width), bf16),
            pltpu.VMEM((owned, width), bf16),
            pltpu.VMEM((n_narrow, owned, width), bf16),
            pltpu.VMEM((n_narrow * owned, width), f32),
            pltpu.VMEM((n_narrow * owned, width), f32),
            pltpu.VMEM((n_narrow, owned, width), bf16),
            pltpu.VMEM((n_narrow, owned, width), bf16),
            pltpu.VMEM((wgu.shape[0], wgu.shape[1] * wgu.shape[2]), bf16),
            pltpu.VMEM(wd.shape, bf16),
            pltpu.VMEM(wgu.shape, bf16),
            pltpu.VMEM((kvw.shape[0], kvw.shape[1] * kvw.shape[2]), bf16),
            dma((n_req,)), dma((n_req,)),
            dma((n_req,)), dma((n_req,)),
            dma((n_req,)), dma((n_req,)),
            dma((n_wide,)), dma((n_wide,)),
            dma((n_narrow,)), dma((n_narrow,)),
            dma((n_narrow,)), dma((n_narrow,)),
            dma((4,)),
        ],
        compiler_params=pltpu.CompilerParams(
            collective_id=cid, has_side_effects=True
        ),
    )(tok, gains, qk_gains, order_pad, wq, kvw, trig, mask16, kv_cache,
      unperm, wout, wgu, wd)

def rms_scale(value_entries, gain_row):
    mean_square = jnp.mean(value_entries * value_entries, axis=-1, keepdims=True)
    return value_entries * lax.rsqrt(mean_square + eps_norm) * gain_row


def rotate(value_entries, position):
    half_width = value_entries.shape[-1] // 2
    frequency = rope_base ** (
        -jnp.arange(half_width, dtype=jnp.float32) * 2.0 / value_entries.shape[-1]
    )
    angles = position[:, None, None] * frequency
    cosines = jnp.cos(angles)
    sines = jnp.sin(angles)
    first_half = value_entries[..., :half_width]
    second_half = value_entries[..., half_width:]
    return jnp.concatenate(
        [first_half * cosines - second_half * sines, second_half * cosines + first_half * sines],
        axis=-1,
    )


def shards(
    tokens,
    gains,
    qk_gains,
    w_query,
    key_value_weight,
    output_weight,
    w_gateup,
    w_down,
    kv_cache,
    lengths,
    page_table,
):
    req_position = lax.axis_index("req")
    kv_position = lax.axis_index("kv")
    hid_position = lax.axis_index("hid")
    req_total = lax.axis_size("req")
    hid_total = lax.axis_size("hid")
    kv_total = lax.axis_size("kv")
    rows_here, _, model_width = tokens.shape
    half_rows = rows_here // kv_total
    head_width = qk_gains.shape[1]
    per_group = w_query.shape[1] // head_width
    pool_size, _, page_size, _ = kv_cache.shape
    request_count = rows_here * req_total
    feature_width = w_query.shape[0]

    own_rows = tokens[:, 0, :]

    group_lengths = lax.dynamic_index_in_dim(lengths, hid_position, axis=1, keepdims=False)
    group_table = lax.dynamic_index_in_dim(page_table, hid_position, axis=1, keepdims=False)
    request_ids = jnp.arange(request_count, dtype=jnp.int32)
    pool_of = (group_table[:, 0] // pool_size) // hid_total
    pool_pos = pool_of * rows_here + request_ids % rows_here
    order = pool_pos[None, :] == request_ids[:, None]
    pad_to = 8 - rows_here
    order_pad = order.reshape(req_total, rows_here, req_total, rows_here)
    order_pad = jnp.pad(order_pad, ((0, 0), (0, pad_to), (0, 0), (0, pad_to)))
    order_pad = order_pad.reshape(8 * req_total, 8 * req_total).astype(jnp.bfloat16)
    unperm = order.T.reshape(request_count, req_total, rows_here)
    unperm = jnp.pad(unperm, ((0, 0), (0, 0), (0, pad_to)))
    unperm = unperm.reshape(request_count, 8 * req_total).astype(jnp.bfloat16)


    mine = lax.dynamic_slice_in_dim(order, req_position * rows_here, rows_here, 0)
    my_lengths = jnp.sum(jnp.where(mine, group_lengths[None, :], 0), axis=1)
    my_tables = jnp.sum(jnp.where(mine[:, :, None], group_table[None, :, :], 0), axis=1)
    position = my_lengths.astype(jnp.float32)
    half_width = head_width // 2
    frequency = rope_base ** (-jnp.arange(half_width, dtype=jnp.float32) * 2.0 / head_width)
    angles = position[:, None] * frequency
    trig = jnp.stack([jnp.cos(angles), jnp.sin(angles)])

    slot_base = (req_position * hid_total + hid_position) * pool_size
    local = my_tables - slot_base
    slots = jnp.arange(pool_size, dtype=jnp.int32)
    match = local[:, :, None] == slots[None, None, :]
    page_ids = jnp.arange(my_tables.shape[1], dtype=jnp.int32)
    owner_hit = jnp.any(match, axis=1)
    page_of = jnp.sum(jnp.where(match, page_ids[None, :, None], 0), axis=(0, 1))
    cache_pos = page_of[:, None] * page_size + jnp.arange(page_size, dtype=jnp.int32)[None, :]
    live = owner_hit[:, :, None] & (cache_pos[None] < my_lengths[:, None, None])
    live = live.reshape(rows_here, pool_size * page_size)
    live = jnp.pad(live, ((0, 0), (0, page_size)))
    mask16 = jnp.tile(live, (per_group, 1)).astype(jnp.int32)

    hidden_width = w_down.shape[0]
    result = layer(
        own_rows,
        gains,
        qk_gains,
        order_pad,
        w_query,
        key_value_weight,
        trig,
        mask16,
        kv_cache,
        unperm,
        output_weight[0],
        w_gateup,
        w_down,
        0,
    )
    return result[:, None, :]


def solution(mesh):
    return jax.shard_map(
        shards,
        mesh=mesh,
        in_specs=(
            P("req", "hid", None),
            P(),
            P(),
            P("req", "kv"),
            P("req", None, "kv"),
            P("kv", "req", None),
            P(None, None, ("kv", "hid")),
            P(("kv", "hid"), None),
            P(("req", "hid"), None, None, "kv"),
            P(),
            P(),
        ),
        out_specs=P(("req", "kv"), "hid", None),
        check_vma=False,
    )
```
